128 devices in a mesh: exp: 4 (over x), tp: 32 (over z, y, core).
Axes of the slice: x: 4, y: 4, z: 4, core: 2. Of those that a mesh axis runs over, the one named last changes fastest.
Arguments:
- inputs: bfloat16 [1024, 4096], P(('exp', 'tp')), may hold values from -6 to 6
- conv_weight: float32 [4, 4096], replicated, may hold values from -3 to 3
- expert_ids: int32 [1024, 2], P(('exp', 'tp')), may hold values from 0 to 7, all different within a row; in each aligned block of 8 rows (0 to 7, 8 to 15, ...) at most 3 rows name the same one
- gate_values: float32 [1024, 2], P(('exp', 'tp')), may hold values from 0.25 to 1
- cotangent: bfloat16 [1024, 4096], P(('exp', 'tp')), may hold values from -6 to 6
- gate_weight: bfloat16 [8, 4096, 14336], P('exp', None, 'tp'), may hold values from -0.09375 to 0.09375
- up_weight: bfloat16 [8, 4096, 14336], P('exp', None, 'tp'), may hold values from -0.09375 to 0.09375
- down_weight: bfloat16 [8, 14336, 4096], P('exp', 'tp'), may hold values from -0.046875 to 0.046875
Outputs:
- result: bfloat16 [1024, 4096], P(('exp', 'tp'))
- grad_inputs: bfloat16 [1024, 4096], P(('exp', 'tp'))
The draws below stay inside these ranges and needn't reach their ends.
Inputs may be any that keep to these rules, and one draw needn't show every extreme that they name: `expert_ids`: the experts of one token differ. Among the 8 tokens of one device no expert is named more than 3 times, a bound that some block reaches; every expert is named somewhere.
All inputs are finite; a program needn't handle non-finite values.
Results may differ from the reference program's by a relative error of at most 0.014.
Values may be sent and summed in bfloat16 or wider, within the bound.
A program may use at most 128 MiB of HBM per device.

```python
import math
import jax
import jax.numpy as jnp
import numpy as np
from jax import lax

D = 4096
FF = 14336
TOP = 2
KW = 4
TOK_DEV = 8
EXPERTS = 8
SLOTS = 3
TOKENS = 1024
N_EXP = 4
N_TP = 32


def level_of(own_key, extent, shards, low, top_value):
    level, own = 1.0, jax.random.fold_in(own_key, 6)
    for position, blocks in shards:
        steps = jnp.exp(jax.random.uniform(jax.random.fold_in(own, position), (blocks,), jnp.float32, low / len(shards), top_value / len(shards)))
        level = level * jnp.repeat(steps, extent[position] // blocks).reshape([-1 if axis == position else 1 for axis in range(len(extent))])
    return level


def deal_out(key, own, number, rows, count, top, bound, lean):
    sequence = jax.random.permutation(key, count)
    packed, common = portions_of(count, rows * top, bound, lean, True), portions_of(count, rows * top, bound, lean, False)
    places = jnp.arange(count)

    def named(sizes, turn):
        used = int((sizes > 0).sum())
        fixed = max(1, used // 4)
        shifted = fixed + (places - fixed + turn * (used - fixed)) % max(1, count - fixed)
        return jnp.zeros((count,), jnp.int32).at[sequence[jnp.where(places < fixed, places, shifted)]].set(jnp.asarray(sizes, jnp.int32))

    sizes = jnp.where(number % 4 == 0, named(packed, number // 4), named(common, number - number // 4 - 1))
    mixed = jax.random.permutation(jax.random.fold_in(own, 3), count)
    giver, receiver = mixed[0:count // 2 * 2:2], mixed[1:count // 2 * 2:2]
    slack = jnp.minimum(sizes[giver] - 1, bound - sizes[receiver]) // 2
    slack = jnp.where((giver == sequence[0]) | (receiver == sequence[0]) | (sizes[receiver] == 0), 0, jnp.maximum(slack, 0))
    shifted = jax.random.randint(jax.random.fold_in(own, 4), (count // 2,), 0, 1 << 20) % (slack + 1)
    sizes = sizes.at[giver].add(-shifted).at[receiver].add(shifted)
    items = jnp.searchsorted(jnp.cumsum(sizes), jnp.arange(rows * top), side="right").astype(jnp.int32)
    table = items.reshape(top, rows).T
    table = table[jax.random.permutation(jax.random.fold_in(own, 1), rows)]
    turn = jax.random.randint(jax.random.fold_in(own, 2), (rows, 1), 0, top)
    return jnp.take_along_axis(table, (jnp.arange(top)[None, :] + turn) % top, axis=1)


def portions_of(count, total, reach, lean, full):
    portions = [(1 << 20) // math.isqrt(rank ** lean) + 1 for rank in range(1, count + 1)]
    largest = reach if full else min(reach, max(-(-total // count), total * portions[0] // sum(portions)))
    least = 1 if total - largest >= count - 1 else 0
    counts, rest = [largest] + [least] * (count - 1), total - largest - least * (count - 1)
    while rest > 0:
        movable = [i for i in range(1, count) if counts[i] < largest] or [i for i in range(1, count) if counts[i] < reach]
        pool, budget = sum([portions[i] for i in movable]), rest
        for i in movable:
            more = min(reach - counts[i], max(1, budget * portions[i] // pool), rest)
            counts[i] = counts[i] + more
            rest = rest - more
    return np.array(counts)


def normal_values(key, dims, width, bound, shards=(), held_as=jnp.bfloat16):
    array = jax.random.normal(key, dims, jnp.float32) * width
    if len(shards) > 0:
        array = level_of(key, dims, shards, -0.22, 0.18) * array
    return jnp.clip(array, min=-bound, max=bound).astype(held_as)


def setup_inputs(seed: int = 0) -> dict:
    key_list = jax.random.split(jax.random.key(seed), 9)
    inputs = normal_values(key_list[0], (TOKENS, D), 1.0, 6.0, ((0, 128),))
    conv_weight = normal_values(key_list[1], (KW, D), 0.5, 3.0, (), jnp.float32)
    expert_ids_keys = jax.random.split(jax.random.fold_in(key_list[2], 1), TOKENS // TOK_DEV)
    expert_ids_turns = jax.random.permutation(jax.random.fold_in(key_list[2], 3), TOKENS // TOK_DEV)
    expert_ids = jax.vmap(lambda own, number: deal_out(jax.random.fold_in(key_list[2], 2), own, number, TOK_DEV, EXPERTS, TOP, SLOTS, 2))(expert_ids_keys, expert_ids_turns).reshape((TOKENS, TOP))
    gate_values = jnp.clip(0.25 + 0.75 * jax.random.uniform(key_list[3], (TOKENS, TOP), jnp.float32) ** level_of(key_list[3], (TOKENS, TOP), ((0, 128),), -0.2, 0.2), 0.25, 1.0)
    cotangent = normal_values(key_list[4], (TOKENS, D), 1.0, 6.0, ((0, 128),))
    gate_weight = normal_values(key_list[5], (EXPERTS, D, FF), D ** -0.5, 0.09375, ((0, 4), (2, 32)))
    up_weight = normal_values(key_list[6], (EXPERTS, D, FF), D ** -0.5, 0.09375, ((0, 4), (2, 32)))
    down_weight = normal_values(key_list[7], (EXPERTS, FF, D), FF ** -0.5, 0.046875, ((0, 4), (1, 32)))
    return {"inputs": inputs, "conv_weight": conv_weight, "expert_ids": expert_ids, "gate_values": gate_values, "cotangent": cotangent, "gate_weight": gate_weight, "up_weight": up_weight, "down_weight": down_weight}


def expert_block(rows_in, rows_grad, gate_block, up_block, down_block):
    gate_pre = jnp.dot(rows_in, gate_block, preferred_element_type=jnp.float32)
    up_pre = jnp.dot(rows_in, up_block, preferred_element_type=jnp.float32)
    sigmoid_gate = jax.nn.sigmoid(gate_pre)
    activated = gate_pre * sigmoid_gate
    hidden = (activated * up_pre).astype(jnp.bfloat16)
    forward_part = jnp.dot(hidden, down_block, preferred_element_type=jnp.float32)
    back_hidden = jnp.dot(rows_grad, down_block.T, preferred_element_type=jnp.float32)
    grad_gate = (back_hidden * up_pre * sigmoid_gate * (1.0 + gate_pre * (1.0 - sigmoid_gate))).astype(jnp.bfloat16)
    grad_up = (back_hidden * activated).astype(jnp.bfloat16)
    backward_part = jnp.dot(grad_gate, gate_block.T, preferred_element_type=jnp.float32) + jnp.dot(grad_up, up_block.T, preferred_element_type=jnp.float32)
    forward_part = lax.optimization_barrier(forward_part.astype(jnp.bfloat16)).astype(jnp.float32)
    backward_part = lax.optimization_barrier(backward_part.astype(jnp.bfloat16)).astype(jnp.float32)
    return forward_part, backward_part


def reference(inputs, conv_weight, expert_ids, gate_values, cotangent, gate_weight, up_weight, down_weight):
    tokens = inputs.shape[0]
    model_width = inputs.shape[1]
    devices = N_EXP * N_TP
    source = inputs.astype(jnp.float32)
    padded = jnp.concatenate([jnp.zeros((KW - 1, model_width), jnp.float32), source], 0)
    conv_sum = source
    for shift_step in range(KW):
        conv_sum = conv_sum + conv_weight[shift_step] * padded[KW - 1 - shift_step:KW - 1 - shift_step + tokens]
    mixed = conv_sum.astype(jnp.bfloat16)

    local_ids = expert_ids.reshape(devices, TOK_DEV * TOP).astype(jnp.int32)
    onehot_ids = (local_ids[:, :, None] == jnp.arange(EXPERTS, dtype=jnp.int32)[None, None, :]).astype(jnp.int32)
    earlier = jnp.cumsum(onehot_ids, 1) - onehot_ids
    slot_index = jnp.sum(earlier * onehot_ids, 2).astype(jnp.int32)
    device_index = jnp.arange(devices, dtype=jnp.int32)[:, None]
    capacity = devices * SLOTS
    row_index = (local_ids * capacity + device_index * SLOTS + slot_index).reshape(-1).astype(jnp.int32)
    token_index = (jnp.arange(tokens * TOP, dtype=jnp.int32) // TOP).astype(jnp.int32)

    buffer_in = jnp.zeros((EXPERTS * capacity, model_width), jnp.bfloat16).at[row_index].set(mixed[token_index])
    buffer_grad = jnp.zeros((EXPERTS * capacity, model_width), jnp.bfloat16).at[row_index].set(cotangent[token_index])
    block_width = FF // N_TP

    def per_expert(operands):
        rows_in, rows_grad, gate_full, up_full, down_full = operands

        def add_block(block_number, totals):
            first_col = (block_number * block_width).astype(jnp.int32)
            gate_block = lax.dynamic_slice_in_dim(gate_full, first_col, block_width, 1)
            up_block = lax.dynamic_slice_in_dim(up_full, first_col, block_width, 1)
            down_block = lax.dynamic_slice_in_dim(down_full, first_col, block_width, 0)
            forward_part, backward_part = expert_block(rows_in, rows_grad, gate_block, up_block, down_block)
            return (totals[0] + forward_part, totals[1] + backward_part)

        empty_sum = jnp.zeros((capacity, model_width), jnp.float32)
        return lax.fori_loop(0, N_TP, add_block, (empty_sum, empty_sum))

    expert_out, expert_back = lax.map(per_expert, (buffer_in.reshape(EXPERTS, capacity, model_width), buffer_grad.reshape(EXPERTS, capacity, model_width), gate_weight, up_weight, down_weight))
    gathered_out = expert_out.reshape(EXPERTS * capacity, model_width)[row_index].reshape(tokens, TOP, model_width)
    gathered_back = expert_back.reshape(EXPERTS * capacity, model_width)[row_index].reshape(tokens, TOP, model_width)
    moe_out = jnp.sum(gathered_out * gate_values[:, :, None], 1)
    moe_back = jnp.sum(gathered_back * gate_values[:, :, None], 1)
    result = (mixed.astype(jnp.float32) + moe_out).astype(jnp.bfloat16)

    grad_mixed = cotangent.astype(jnp.float32) + moe_back
    padded_grad = jnp.concatenate([grad_mixed, jnp.zeros((KW - 1, model_width), jnp.float32)], 0)
    grad_sum = grad_mixed
    for shift_step in range(KW):
        grad_sum = grad_sum + conv_weight[shift_step] * padded_grad[shift_step:shift_step + tokens]
    return result, grad_sum.astype(jnp.bfloat16)
```

```python
import jax
import jax.numpy as jnp
import ml_dtypes
import numpy as np
from jax import lax
from jax.experimental import pallas as pl
from jax.experimental.pallas import tpu as pltpu
from jax.sharding import PartitionSpec as P

MESH = pl.DeviceIdType.MESH
BF16, F32 = jnp.bfloat16, jnp.float32
RING = 4
CORES = 2
SLOTS = 3
PEERS = 8
ROWS = PEERS * SLOTS
CHUNKS = 4
NT = (((1,), (1,)), ((), ()))


def moe_kernel(
    mc, disp, sel, ret, gates, gw, uw, dw, out,
    pk, xr, buf, wgu, wd, lhs, acc_gu, acc_b, hid, gg,
    res, rel, ful, part, rel2, ful2, fin, pk2, yr,
    w_local, w_send, w_recv, x_send, x_recv, g_send, g_recv, r_send, r_recv, y_send, y_recv,
):
    width = mc.shape[1]
    dc = width // CHUNKS
    half = dc // 2
    f = gw.shape[1]
    rows = RING * RING * ROWS
    x, t = lax.axis_index("exp"), lax.axis_index("tp")
    z, y, c = t // (RING * CORES), (t // CORES) % RING, t % CORES
    q = x * CORES + c
    sent = []

    def device(x, z, y, c):
        return (x, (z * RING + y) * CORES + c)

    def step_y(by):
        return device(x, z, (y + by) % RING, c)

    def step_z(by):
        return device(x, (z + by) % RING, y, c)

    first, second = (y, z), (z, y)
    step_first, step_second = (step_y, step_z), (step_z, step_y)

    def remote(src, dst, send_sem, recv_sem, to):
        copy = pltpu.make_async_remote_copy(
            src_ref=src, dst_ref=dst, send_sem=send_sem, recv_sem=recv_sem,
            device_id=to, device_id_type=MESH,
        )
        copy.start()
        sent.append(copy)
        return copy

    peers = []
    for dx in range(PEERS // CORES):
        for dcore in range(CORES):
            if dx or dcore:
                px, pc = (x + dx) % (PEERS // CORES), (c + dcore) % CORES
                peers.append((dx * CORES + dcore, px * CORES + pc, device(px, z, y, pc)))
    barrier = pltpu.get_barrier_semaphore()
    partners = [to for _, _, to in peers] + [s(by) for s in step_first for by in (1, -1)]
    for to in partners:
        pl.semaphore_signal(barrier, inc=1, device_id=to, device_id_type=MESH)

    for k in range(CHUNKS):
        cols = pl.ds(k * dc, dc)
        packed = jnp.dot(disp[...], mc[:, cols], preferred_element_type=F32)
        pk[:, :, cols] = packed.reshape(PEERS, 8, dc).astype(BF16)
    pl.semaphore_wait(barrier, len(partners))

    exchanged = {}
    for k in range(CHUNKS):
        cols = pl.ds(k * dc, dc)
        for n, p, to in peers:
            exchanged[k, n] = remote(
                pk.at[p, :, cols], xr.at[q, :, cols], x_send.at[k, n], x_recv.at[k, n], to
            )
    xr[q] = pk[q]

    sibling = device(x, z, y, 1 - c)
    weights, swapped = [], []
    for n, (w, into, at) in enumerate(((gw, wgu, 0), (uw, wgu, 2 * f), (dw, wd, 0))):
        copy = pltpu.make_async_copy(w.at[c], into.at[pl.ds(at, f)], w_local.at[n])
        copy.start()
        weights.append(copy)
        swapped.append(
            remote(w.at[1 - c], into.at[pl.ds(at + f, f)], w_send.at[n], w_recv.at[n], sibling)
        )

    gathering = {}

    def gather_view(a, k, phase, j, h=None):
        if phase == 0:
            v = buf.at[a, k, second[a], j]
            return v if h is None else v.at[:, pl.ds(h * half, half)]
        v = buf.at[a, k, j]
        return v if h is None else v.at[pl.ds(h * 2, 2)]

    def gather_send(k, phase):
        for a in range(2):
            own, to = (first, second)[phase][a], (step_first, step_second)[phase][a]
            v = gather_view(a, k, phase, own)
            for m, by in ((0, 1), (1, -1)):
                gathering[a, k, phase, m] = remote(
                    v, v, g_send.at[a, k, phase, m], g_recv.at[a, k, phase, m], to(by)
                )

    def gather_relay(k, phase):
        for a in range(2):
            own, to = (first, second)[phase][a], (step_first, step_second)[phase][a]
            for m, by in ((0, 1), (1, -1)):
                gathering[a, k, phase, m].wait_recv()
                v = gather_view(a, k, phase, (own - by) % RING, m)
                gathering[a, k, phase, m + 2] = remote(
                    v, v, g_send.at[a, k, phase, m + 2], g_recv.at[a, k, phase, m + 2], to(by)
                )

    def gather_wait(k, phase):
        for a in range(2):
            for m in (2, 3):
                gathering[a, k, phase, m].wait_recv()

    def select(k):
        cols = pl.ds(k * dc, dc)
        for n, _, _ in peers:
            exchanged[k, n].wait_recv()
        got = xr[:, :, cols].astype(F32).reshape(PEERS * 8, dc).astype(BF16)
        own = jnp.dot(sel[...], got, preferred_element_type=F32)
        for a in range(2):
            buf[a, k, second[a], first[a]] = own[a * ROWS : (a + 1) * ROWS].astype(BF16)

    def products(k):
        slab = RING * ROWS
        for s in range(RING):
            for a, v in ((0, buf[0, k, s]), (1, buf[1, k, :, s])):
                lhs[a, s * slab : (s + 1) * slab] = v.astype(F32).reshape(slab, dc).astype(BF16)
        cols = pl.ds(k * dc, dc)

        def add(acc, a, w, at, n):
            made = lax.dot_general(lhs[a], w[pl.ds(at, n), cols], NT, preferred_element_type=F32)
            acc[:, pl.ds(at, n)] = made if k == 0 else acc[:, pl.ds(at, n)] + made

        def tile(i, carry):
            add(acc_gu, 0, wgu, pl.multiple_of(i * 256, 256), 256)
            return carry

        lax.fori_loop(0, 4 * f // 256, tile, 0)

        def tile_b(i, carry):
            add(acc_b, 1, wd, pl.multiple_of(i * 256, 256), 256)
            return carry

        lax.fori_loop(0, 2 * f // 256, tile_b, 0)
        if 2 * f % 256:
            add(acc_b, 1, wd, 2 * f // 256 * 256, 2 * f % 256)

    def activate():
        def strip(i, carry):
            r = pl.ds(pl.multiple_of(i * 16, 16), 16)
            gate_pre, up_pre = acc_gu[r, : 2 * f], acc_gu[r, 2 * f :]
            back = acc_b[r, :]
            s = jax.nn.sigmoid(gate_pre)
            silu = gate_pre * s
            hid[r, :] = (silu * up_pre).astype(BF16)
            gg[r, : 2 * f] = (back * up_pre * s * (1.0 + gate_pre * (1.0 - s))).astype(BF16)
            gg[r, 2 * f :] = (back * silu).astype(BF16)
            return carry

        lax.fori_loop(0, rows // 16, strip, 0)

    def outputs(k):
        def tile(i, carry):
            at = pl.multiple_of(i * 256, 256)
            cols = pl.ds(k * dc + at, 256)
            forward = jnp.dot(hid[...], wd[:, cols], preferred_element_type=F32)
            res[0, k, :, :, :, pl.ds(at, 256)] = forward.reshape(RING, RING, ROWS, 256).astype(BF16)
            backward = jnp.dot(gg[...], wgu[:, cols], preferred_element_type=F32)
            backward = backward.reshape(RING, RING, ROWS, 256).astype(BF16)
            for s in range(RING):
                res[1, k, :, s, :, pl.ds(at, 256)] = backward[s]
            return carry

        lax.fori_loop(0, dc // 256, tile, 0)

    reducing = {}

    def partial(a, k, phase, j, h=None):
        if phase == 0:
            v = res.at[a, k, j]
            return v if h is None else v.at[pl.ds(h * 2, 2)]
        v = part.at[a, k, j]
        return v if h is None else v.at[:, pl.ds(h * half, half)]

    def reduce_relay(k, phase):
        for a in range(2):
            own, to = (second, first)[phase][a], (step_second, step_first)[phase][a]
            for m, by in ((0, 1), (1, -1)):
                reducing[a, k, phase, m] = remote(
                    partial(a, k, phase, (own + 2) % RING, m), (rel, rel2)[phase].at[a, k, m],
                    r_send.at[a, k, phase, m], r_recv.at[a, k, phase, m], to(by),
                )

    def reduce_send(k, phase):
        for a in range(2):
            own, to = (second, first)[phase][a], (step_second, step_first)[phase][a]
            for m, by in ((0, 1), (1, -1)):
                reducing[a, k, phase, m].wait_recv()
                j = (own + by) % RING
                mine, came = partial(a, k, phase, j, m), (rel, rel2)[phase]
                mine[...] = (mine[...].astype(F32) + came[a, k, m].astype(F32)).astype(BF16)
                reducing[a, k, phase, m + 2] = remote(
                    partial(a, k, phase, j), (ful, ful2)[phase].at[a, k, m],
                    r_send.at[a, k, phase, m + 2], r_recv.at[a, k, phase, m + 2], to(by),
                )

    def reduce_sum(k, phase):
        for a in range(2):
            own = (second, first)[phase][a]
            for m in (2, 3):
                reducing[a, k, phase, m].wait_recv()
            came = (ful, ful2)[phase]
            total = partial(a, k, phase, own)[...].astype(F32)
            total = total + came[a, k, 0].astype(F32) + came[a, k, 1].astype(F32)
            if phase == 0:
                part[a, k] = total.astype(BF16)
            else:
                fin[a * ROWS : (a + 1) * ROWS, :] = total

    returned = {}

    def give_back(k):
        cols = pl.ds(k * dc, dc)
        packed = jnp.dot(ret[...], fin[...].astype(BF16), preferred_element_type=F32)
        pk2[:, :, cols] = packed.reshape(PEERS, 8, dc).astype(BF16)
        for n, p, to in peers:
            returned[k, n] = remote(
                pk2.at[p, :, cols], yr.at[q, :, cols], y_send.at[k, n], y_recv.at[k, n], to
            )
        yr[q, :, cols] = pk2[q, :, cols]

    def combine(k):
        cols = pl.ds(k * dc, dc)
        for n, _, _ in peers:
            returned[k, n].wait_recv()
        got = yr[:, :, cols].astype(F32).reshape(PEERS * 8, dc)
        out[:, cols] = jnp.dot(
            gates[...], got, preferred_element_type=F32, precision=lax.Precision.HIGHEST
        )

    def gather_start(k):
        gather_wait(k, 0)
        gather_send(k, 1)

    def gather_end(k):
        gather_wait(k, 1)
        products(k)

    def reduce_next(k):
        reduce_sum(k, 0)
        reduce_relay(k, 1)

    def reduce_end(k):
        reduce_sum(k, 1)
        give_back(k)

    for k in range(CHUNKS):
        select(k)
        gather_send(k, 0)
        if k >= 1:
            gather_relay(k - 1, 0)
        if k >= 2:
            gather_start(k - 2)
    gather_relay(CHUNKS - 1, 0)
    for k in range(CHUNKS):
        gather_relay(k, 1)
        if k + 2 < CHUNKS:
            gather_start(k + 2)
        if k == 0:
            for copy in weights:
                copy.wait()
            for copy in swapped:
                copy.wait_recv()
        else:
            gather_end(k - 1)
    gather_end(CHUNKS - 1)
    activate()
    for s in range(CHUNKS + 4):
        if s < CHUNKS:
            outputs(s)
            reduce_relay(s, 0)
        if 0 <= s - 1 < CHUNKS:
            reduce_send(s - 1, 0)
        if 0 <= s - 2 < CHUNKS:
            reduce_next(s - 2)
        if 0 <= s - 3 < CHUNKS:
            reduce_send(s - 3, 1)
        if 0 <= s - 4 < CHUNKS:
            reduce_end(s - 4)
    for k in range(CHUNKS):
        combine(k)
    for copy in sent:
        copy.wait_send()


def moe(mc, disp, sel, ret, gates, gw, uw, dw):
    width, f = mc.shape[1], gw.shape[1]
    dc = width // CHUNKS
    rows = RING * RING * ROWS
    vmem = pl.BlockSpec(memory_space=pltpu.VMEM)
    hbm = pl.BlockSpec(memory_space=pl.ANY)
    dma = pltpu.SemaphoreType.DMA
    flops = 6 * 2 * rows * width * 2 * f
    return pl.pallas_call(
        moe_kernel,
        out_shape=jax.ShapeDtypeStruct((16, width), F32),
        in_specs=[vmem] * 5 + [hbm] * 3,
        out_specs=vmem,
        scratch_shapes=[
            pltpu.VMEM((PEERS, 8, width), BF16),
            pltpu.VMEM((PEERS, 8, width), BF16),
            pltpu.VMEM((2, CHUNKS, RING, RING, ROWS, dc), BF16),
            pltpu.VMEM((4 * f, width), BF16),
            pltpu.VMEM((2 * f, width), BF16),
            pltpu.VMEM((2, rows, dc), BF16),
            pltpu.VMEM((rows, 4 * f), F32),
            pltpu.VMEM((rows, 2 * f), F32),
            pltpu.VMEM((rows, 2 * f), BF16),
            pltpu.VMEM((rows, 4 * f), BF16),
            pltpu.VMEM((2, CHUNKS, RING, RING, ROWS, dc), BF16),
            pltpu.VMEM((2, CHUNKS, 2, 2, ROWS, dc), BF16),
            pltpu.VMEM((2, CHUNKS, 2, RING, ROWS, dc), BF16),
            pltpu.VMEM((2, CHUNKS, RING, ROWS, dc), BF16),
            pltpu.VMEM((2, CHUNKS, 2, ROWS, dc // 2), BF16),
            pltpu.VMEM((2, CHUNKS, 2, ROWS, dc), BF16),
            pltpu.VMEM((2 * ROWS, dc), F32),
            pltpu.VMEM((PEERS, 8, width), BF16),
            pltpu.VMEM((PEERS, 8, width), BF16),
            dma((3,)),
            dma((3,)),
            dma((3,)),
            dma((CHUNKS, PEERS)),
            dma((CHUNKS, PEERS)),
            dma((2, CHUNKS, 2, 4)),
            dma((2, CHUNKS, 2, 4)),
            dma((2, CHUNKS, 2, 4)),
            dma((2, CHUNKS, 2, 4)),
            dma((CHUNKS, PEERS)),
            dma((CHUNKS, PEERS)),
        ],
        compiler_params=pltpu.CompilerParams(
            collective_id=0, has_side_effects=True, vmem_limit_bytes=58 << 20
        ),
        cost_estimate=pl.CostEstimate(
            flops=flops, bytes_accessed=12 * f * width, transcendentals=rows * 2 * f
        ),
    )(mc, disp, sel, ret, gates, gw, uw, dw)


def shifted(array, axis, by):
    size = lax.axis_size(axis)
    pairs = [(i, i + by) for i in range(size) if 0 <= i + by < size]
    return lax.ppermute(array, axis, pairs)


def row_maps():
    sel = np.zeros((2 * ROWS, PEERS * 8), ml_dtypes.bfloat16)
    for a in range(2):
        for s in range(PEERS):
            for n in range(SLOTS):
                sel[a * ROWS + s * SLOTS + n, s * 8 + a * SLOTS + n] = 1
    return jnp.asarray(sel), jnp.asarray(sel.T.copy())


def per_device(
    inputs, conv_weight, expert_ids, gate_values, cotangent, gate_weight, up_weight, down_weight
):
    tok_rows = inputs.shape[0]
    kernel = conv_weight.shape[0]
    source = inputs.astype(F32)
    rim_rows = shifted(inputs[tok_rows - (kernel - 1) :], ("exp", "tp"), 1)
    extended = jnp.concatenate([rim_rows.astype(F32), source], 0)
    conv_sum = source
    for j in range(kernel):
        conv_sum = conv_sum + conv_weight[j] * extended[kernel - 1 - j : kernel - 1 - j + tok_rows]
    mixed = conv_sum.astype(BF16)

    flat_ids = expert_ids.reshape(-1)
    order = jnp.arange(flat_ids.shape[0])
    same = (flat_ids[:, None] == flat_ids[None, :]) & (order[None, :] < order[:, None])
    slot = jnp.sum(same.astype(jnp.int32), 1).reshape(expert_ids.shape)
    target = expert_ids * 8 + slot
    places = jnp.arange(PEERS * 8, dtype=jnp.int32)
    hit_in = places[None, None, :] == target[:, :, None]
    hit_grad = places[None, None, :] == target[:, :, None] + SLOTS
    disp = jnp.concatenate([jnp.any(hit_in, 1), jnp.any(hit_grad, 1)], 0).astype(BF16).T
    gates = jnp.concatenate(
        [jnp.sum(jnp.where(hit, gate_values[:, :, None], 0.0), 1) for hit in (hit_in, hit_grad)], 0
    )
    sel, ret = row_maps()
    moe_sums = moe(
        jnp.concatenate([mixed, cotangent], 0), disp, sel, ret, gates,
        jnp.swapaxes(gate_weight, 1, 2), jnp.swapaxes(up_weight, 1, 2), down_weight,
    )
    result = (mixed.astype(F32) + moe_sums[:tok_rows]).astype(BF16)
    grad_mixed = cotangent.astype(F32) + moe_sums[tok_rows:]
    next_rows = shifted(grad_mixed[: kernel - 1].astype(BF16), ("exp", "tp"), -1).astype(F32)
    extended_grad = jnp.concatenate([grad_mixed, next_rows], 0)
    grad_sum = grad_mixed
    for j in range(kernel):
        grad_sum = grad_sum + conv_weight[j] * extended_grad[j : j + tok_rows]
    return (result, grad_sum.astype(BF16))


def solution(mesh):
    in_specs = (
        P(("exp", "tp"), None),
        P(),
        P(("exp", "tp"), None),
        P(("exp", "tp"), None),
        P(("exp", "tp"), None),
        P("exp", None, "tp"),
        P("exp", None, "tp"),
        P("exp", "tp", None),
    )
    out_specs = (P(("exp", "tp"), None), P(("exp", "tp"), None))
    return jax.shard_map(
        per_device, mesh=mesh, in_specs=in_specs, out_specs=out_specs, check_vma=False
    )
```

```python
import jax
import jax.numpy as jnp
import ml_dtypes
import numpy as np
from jax import lax
from jax.experimental import pallas as pl
from jax.experimental.pallas import tpu as pltpu
from jax.sharding import PartitionSpec as P

MESH = pl.DeviceIdType.MESH
BF16, F32 = jnp.bfloat16, jnp.float32
RING = 4
PLANE = RING * RING
CORES = 2
SLOTS = 3
PEERS = 8
BLOCK = 4
TAPS = 4
GROUPS = ((2, 4), (1, 2))
UNITS = [(g, k) for g, (_, pieces) in enumerate(GROUPS) for k in range(pieces)]
NT = (((1,), (1,)), ((), ()))


def moe_kernel(
    inputs, conv, ids, gate_values, cot, sel, ret, gw, uw, dw, result, grad,
    ext, halo_out, halo_in, back_out, back_in, mixed, gates, pk, xr, pk2, yr, wgu, wd, *rest,
):
    per_group, sems = rest[: 13 * len(GROUPS)], rest[13 * len(GROUPS) :]
    buf, lhs, acc_gu, acc_b, hid, gg, res, rel, ful, part, rel2, ful2, fin = (
        per_group[i * len(GROUPS) : (i + 1) * len(GROUPS)] for i in range(13)
    )
    w_sem, h_sem, b_sem, x_send, x_recv, g_send, g_recv, r_send, r_recv, y_send, y_recv = sems
    width = inputs.shape[1]
    f = gw.shape[1]

    x, t = lax.axis_index("exp"), lax.axis_index("tp")
    n_exp, n_tp = PEERS // CORES, PLANE * CORES
    z, y, c = t // (RING * CORES), (t // CORES) % RING, t % CORES
    q = x * CORES + c
    here, devices = x * n_tp + t, n_exp * n_tp

    def rows_of(g):
        return PEERS * GROUPS[g][0]

    def cols_of(u):
        g, k = UNITS[u]
        dc = width // GROUPS[g][1]
        return pl.ds(k * dc, dc)

    def device(x, z, y, c):
        return (x, (z * RING + y) * CORES + c)

    def step_y(by):
        return device(x, z, (y + by) % RING, c)

    def step_z(by):
        return device(x, (z + by) % RING, y, c)

    def line(by):
        v = (here + by) % devices
        return (v // n_tp, v % n_tp)

    axes = ((y, z), (z, y))
    steps = ((step_y, step_z), (step_z, step_y))
    place = [axes[a][1] * RING + axes[a][0] for a in range(2)]

    def remote(src, dst, send_sem, recv_sem, to):
        pltpu.make_async_remote_copy(
            src_ref=src, dst_ref=dst, send_sem=send_sem, recv_sem=recv_sem,
            device_id=to, device_id_type=MESH,
        ).start()

    def wait(sem, like):
        pltpu.make_async_copy(like, like, sem).wait()

    peers = []
    for dx in range(n_exp):
        for dcore in range(CORES):
            if dx or dcore:
                px, pc = (x + dx) % n_exp, (c + dcore) % CORES
                peers.append((px * CORES + pc, device(px, z, y, pc)))
    barrier = pltpu.get_barrier_semaphore()
    partners = [to for _, to in peers] + [s(by) for s in steps[0] for by in (1, -1)]
    partners += [line(1), line(-1)]
    for to in partners:
        pl.semaphore_signal(barrier, inc=1, device_id=to, device_id_type=MESH)

    own = inputs[...].astype(F32)
    ext[8:16, :] = own
    halo_out[...] = own[4:8].astype(BF16)

    r = lax.broadcasted_iota(jnp.int32, (PEERS * 8, 8), 0)
    expert, row = r >> 3, r & 7
    before = lax.broadcasted_iota(jnp.int32, (8, 8), 0) < lax.broadcasted_iota(jnp.int32, (8, 8), 1)
    named = [(expert == ids[k : k + 1, :]).astype(F32) for k in range(2)]
    earlier = jnp.dot(named[0] + named[1], before.astype(F32), preferred_element_type=F32)
    at = [
        jnp.where(row == 4, 2, jnp.where(row < 2, row, -1)),
        jnp.where(row == 5, 2, jnp.where((row == 2) | (row == 3), row - 2, -1)),
    ]
    hit = [(earlier == at[a].astype(F32)).astype(F32) for a in range(2)]
    disp = [((named[0] + named[1]) * hit[a]).astype(BF16) for a in range(2)]
    gate = named[0] * gate_values[0:1, :] + named[1] * gate_values[1:2, :]
    same = lax.broadcasted_iota(jnp.int32, (8, 8), 0) == lax.broadcasted_iota(jnp.int32, (8, 8), 1)
    for a in range(2):
        gates[a * 8 : (a + 1) * 8, :] = lax.dot_general(
            same.astype(F32), gate * hit[a], NT,
            preferred_element_type=F32, precision=lax.Precision.HIGHEST,
        )

    pl.semaphore_wait(barrier, len(partners))
    remote(halo_out, halo_in, h_sem.at[0], h_sem.at[1], line(1))
    wait(h_sem.at[1], halo_in)
    ext[4:8, :] = jnp.where(here == 0, 0.0, halo_in[...].astype(F32))
    total = own
    for j in range(TAPS):
        total = total + conv[j : j + 1, :] * ext[8 - j : 16 - j, :]
    mixed[...] = total.astype(BF16)
    packed = jnp.dot(disp[0], mixed[...], preferred_element_type=F32)
    packed = packed + jnp.dot(disp[1], cot[...], preferred_element_type=F32)
    packed = packed.reshape(PEERS, 8, width)
    pk[0] = packed[:, :BLOCK].astype(BF16)
    pk[1] = packed[:, BLOCK:].astype(BF16)

    for u, (g, _) in enumerate(UNITS):
        cols = cols_of(u)
        for p, to in peers:
            remote(pk.at[g, p, :, cols], xr.at[g, q, :, cols], x_send.at[u], x_recv.at[u], to)
    for g in range(len(GROUPS)):
        xr[g, q] = pk[g, q]

    sibling = device(x, z, y, 1 - c)
    for w, into, first in ((gw, wgu, 0), (uw, wgu, 2 * f), (dw, wd, 0)):
        pltpu.make_async_copy(w.at[c], into.at[pl.ds(first, f)], w_sem.at[0]).start()
        remote(
            w.at[1 - c], into.at[pl.ds(first + f, f)], w_sem.at[1], w_sem.at[2], sibling
        )

    def gather_view(a, u, phase, j, h=None):
        g, k = UNITS[u]
        if phase == 0:
            v = buf[g].at[a, k, axes[a][1] * RING + j]
            half = width // GROUPS[g][1] // 2
            return v if h is None else v.at[:, pl.ds(h * half, half)]
        return buf[g].at[a, k, pl.ds(j * RING, RING) if h is None else pl.ds(j * RING + 2 * h, 2)]

    def blocks(u, n):
        g, k = UNITS[u]
        return buf[g].at[0, k, pl.ds(0, n)]

    def gather_send(u, phase):
        for a in range(2):
            v = gather_view(a, u, phase, axes[a][phase])
            for by in (1, -1):
                remote(v, v, g_send.at[u], g_recv.at[u, phase, 0], steps[a][phase](by))

    def gather_relay(u, phase):
        wait(g_recv.at[u, phase, 0], blocks(u, (4, 16)[phase]))
        for a in range(2):
            for h, by in ((0, 1), (1, -1)):
                v = gather_view(a, u, phase, (axes[a][phase] - by) % RING, h)
                remote(v, v, g_send.at[u], g_recv.at[u, phase, 1], steps[a][phase](by))

    def gather_wait(u, phase):
        wait(g_recv.at[u, phase, 1], blocks(u, (2, 8)[phase]))

    def select(u):
        g, k = UNITS[u]
        cols, n = cols_of(u), rows_of(g)
        wait(x_recv.at[u], xr.at[g, pl.ds(0, PEERS - 1), :, cols])
        got = xr[g, :, :, cols].astype(F32)
        got = jnp.concatenate([got, jnp.zeros_like(got)], 1)
        got = got.reshape(PEERS * 8, got.shape[-1]).astype(BF16)
        first = sum(2 * rows_of(i) for i in range(g))
        mine = jnp.dot(sel[first : first + 2 * n, :], got, preferred_element_type=F32)
        for a in range(2):
            buf[g][a, k, place[a]] = mine[a * n : (a + 1) * n].astype(BF16)

    def products(u):
        g, k = UNITS[u]
        n, cols = rows_of(g), cols_of(u)
        dc, slab = width // GROUPS[g][1], RING * rows_of(g)
        for s in range(RING):
            v = buf[g][0, k, s * RING : (s + 1) * RING].astype(F32)
            lhs[g][0, s * slab : (s + 1) * slab] = v.reshape(slab, dc).astype(BF16)
            v = jnp.stack([buf[g][1, k, j * RING + s] for j in range(RING)], 0).astype(F32)
            lhs[g][1, s * slab : (s + 1) * slab] = v.reshape(slab, dc).astype(BF16)

        def add(acc, a, w, at, n):
            made = lax.dot_general(
                lhs[g][a], w[pl.ds(at, n), cols], NT, preferred_element_type=F32
            )
            acc[:, pl.ds(at, n)] = made if k == 0 else acc[:, pl.ds(at, n)] + made

        def tile(i, carry):
            add(acc_gu[g], 0, wgu, pl.multiple_of(i * 256, 256), 256)
            return carry

        lax.fori_loop(0, 4 * f // 256, tile, 0)

        def tile_b(i, carry):
            add(acc_b[g], 1, wd, pl.multiple_of(i * 256, 256), 256)
            return carry

        lax.fori_loop(0, 2 * f // 256, tile_b, 0)
        if 2 * f % 256:
            add(acc_b[g], 1, wd, 2 * f // 256 * 256, 2 * f % 256)

    def activate(g):
        def strip(i, carry):
            r = pl.ds(pl.multiple_of(i * 16, 16), 16)
            gate_pre, up_pre = acc_gu[g][r, : 2 * f], acc_gu[g][r, 2 * f :]
            back = acc_b[g][r, :]
            s = jax.nn.sigmoid(gate_pre)
            silu = gate_pre * s
            hid[g][r, :] = (silu * up_pre).astype(BF16)
            gg[g][r, : 2 * f] = (back * up_pre * s * (1.0 + gate_pre * (1.0 - s))).astype(BF16)
            gg[g][r, 2 * f :] = (back * silu).astype(BF16)
            return carry

        lax.fori_loop(0, PLANE * rows_of(g) // 16, strip, 0)

    def outputs(u):
        g, k = UNITS[u]
        n, dc = rows_of(g), width // GROUPS[g][1]

        def tile(i, carry):
            at = pl.multiple_of(i * 256, 256)
            cols, to = pl.ds(k * dc + at, 256), pl.ds(at, 256)
            forward = jnp.dot(hid[g][...], wd[:, cols], preferred_element_type=F32)
            res[g][0, k, :, :, to] = forward.reshape(PLANE, n, 256).astype(BF16)
            backward = jnp.dot(gg[g][...], wgu[:, cols], preferred_element_type=F32)
            backward = backward.reshape(RING, RING, n, 256).astype(BF16)
            for s in range(RING):
                res[g][1, k, s * RING : (s + 1) * RING, :, to] = backward[:, s]
            return carry

        lax.fori_loop(0, dc // 256, tile, 0)

    def partial(a, u, phase, j, h=None):
        g, k = UNITS[u]
        if phase == 0:
            return res[g].at[
                a, k, pl.ds(j * RING, RING) if h is None else pl.ds(j * RING + 2 * h, 2)
            ]
        v = part[g].at[a, k, j]
        half = width // GROUPS[g][1] // 2
        return v if h is None else v.at[:, pl.ds(h * half, half)]

    def reduce_relay(u, phase):
        g, k = UNITS[u]
        for a in range(2):
            own, to = axes[a][1 - phase], steps[a][1 - phase]
            for h, by in ((0, 1), (1, -1)):
                remote(
                    partial(a, u, phase, (own + 2) % RING, h), (rel, rel2)[phase][g].at[a, k, h],
                    r_send.at[u], r_recv.at[u, phase, 0], to(by),
                )

    def reduce_send(u, phase):
        g, k = UNITS[u]
        wait(r_recv.at[u, phase, 0], blocks(u, (8, 2)[phase]))
        for a in range(2):
            own, to = axes[a][1 - phase], steps[a][1 - phase]
            for h, by in ((0, 1), (1, -1)):
                j = (own + by) % RING
                mine, came = partial(a, u, phase, j, h), (rel, rel2)[phase][g]
                mine[...] = (mine[...].astype(F32) + came[a, k, h].astype(F32)).astype(BF16)
                remote(
                    partial(a, u, phase, j), (ful, ful2)[phase][g].at[a, k, h],
                    r_send.at[u], r_recv.at[u, phase, 1], to(by),
                )

    def reduce_sum(u, phase):
        g, k = UNITS[u]
        n = rows_of(g)
        wait(r_recv.at[u, phase, 1], blocks(u, (16, 4)[phase]))
        for a in range(2):
            came = (ful, ful2)[phase][g]
            total = partial(a, u, phase, axes[a][1 - phase])[...].astype(F32)
            total = total + came[a, k, 0].astype(F32) + came[a, k, 1].astype(F32)
            if phase == 0:
                part[g][a, k] = total.astype(BF16)
            else:
                fin[g][a * n : (a + 1) * n, :] = total

    def give_back(u):
        g, _ = UNITS[u]
        cols, n = cols_of(u), 2 * rows_of(g)
        back = ret[g * PEERS * 8 : (g + 1) * PEERS * 8, :n]
        packed = jnp.dot(back, fin[g][...].astype(BF16), preferred_element_type=F32)
        packed = packed.reshape(PEERS, 8, packed.shape[-1])[:, :BLOCK].astype(BF16)
        pk2[g, :, :, cols] = packed
        for p, to in peers:
            remote(pk2.at[g, p, :, cols], yr.at[g, q, :, cols], y_send.at[u], y_recv.at[u], to)
        yr[g, q, :, cols] = pk2[g, q, :, cols]

    parts = min(pieces for _, pieces in GROUPS)
    span = width // parts

    def combine(i):
        cols = pl.ds(i * span, span)
        for u, (g, k) in enumerate(UNITS):
            if k * parts // GROUPS[g][1] == i:
                wait(y_recv.at[u], yr.at[g, pl.ds(0, PEERS - 1), :, cols_of(u)])
        got = [yr[g, :, :, cols].astype(F32) for g in range(len(GROUPS))]
        got = jnp.concatenate(got, 1).reshape(PEERS * 8, span)
        sums = jnp.dot(
            gates[...], got, preferred_element_type=F32, precision=lax.Precision.HIGHEST
        )
        result[:, cols] = (mixed[:, cols].astype(F32) + sums[:8]).astype(BF16)
        grad_mixed = cot[:, cols].astype(F32) + sums[8:]
        ext[0:8, cols] = grad_mixed
        back_out[:, cols] = grad_mixed[:4].astype(BF16)
        remote(
            back_out.at[:, cols], back_in.at[:, cols], b_sem.at[0, i], b_sem.at[1, i], line(-1)
        )

    def finish(i):
        cols = pl.ds(i * span, span)
        wait(b_sem.at[1, i], back_in.at[:, cols])
        ext[8:12, cols] = jnp.where(here == devices - 1, 0.0, back_in[:, cols].astype(F32))
        total = ext[0:8, cols]
        for j in range(TAPS):
            total = total + conv[j : j + 1, cols] * ext[j : j + 8, cols]
        grad[:, cols] = total.astype(BF16)

    n = len(UNITS)
    last = GROUPS[0][1] - 1

    def gather_step(s):
        if s < n:
            select(s)
            gather_send(s, 0)
        if 0 <= s - 1 < n:
            gather_relay(s - 1, 0)
        if 0 <= s - 4 < n:
            gather_relay(s - 4, 1)
        if 0 <= s - 2 < n:
            gather_wait(s - 2, 0)
            gather_send(s - 2, 1)

    def gather_end(u):
        if u == 0:
            wait(w_sem.at[0], wgu.at[pl.ds(0, 3 * f)])
            wait(w_sem.at[2], wgu.at[pl.ds(0, 3 * f)])
        gather_wait(u, 1)
        products(u)
        g, k = UNITS[u]
        if k + 1 == GROUPS[g][1]:
            activate(g)

    def reduce_step(s):
        if s < n:
            outputs(s)
            reduce_relay(s, 0)
        if 0 <= s - 1 < n:
            reduce_send(s - 1, 0)
        if 0 <= s - 2 < n:
            reduce_sum(s - 2, 0)
            reduce_relay(s - 2, 1)
        if 0 <= s - 3 < n:
            reduce_send(s - 3, 1)
        if 0 <= s - 4 < n:
            reduce_sum(s - 4, 1)
            give_back(s - 4)

    for s in range(last + 6):
        gather_step(s)
        if s >= 5:
            gather_end(s - 5)
    for s in range(n + 4):
        reduce_step(s)
        if last + 6 + s < n + 5:
            gather_step(last + 6 + s)
            gather_end(last + 1 + s)
    for i in range(parts):
        combine(i)
    for i in range(parts):
        finish(i)

    wait(h_sem.at[0], halo_out)
    wait(w_sem.at[1], wgu.at[pl.ds(0, 3 * f)])
    for i in range(parts):
        wait(b_sem.at[0, i], back_out.at[:, pl.ds(i * span, span)])
    for u, (g, k) in enumerate(UNITS):
        wait(x_send.at[u], xr.at[g, pl.ds(0, PEERS - 1), :, cols_of(u)])
        wait(y_send.at[u], yr.at[g, pl.ds(0, PEERS - 1), :, cols_of(u)])
        wait(g_send.at[u], buf[g].at[:, k, pl.ds(0, PLANE - 1)])
        wait(r_send.at[u], res[g].at[:, k, pl.ds(0, PLANE - 1)])


def moe(inputs, conv, ids, gate_values, cot, sel, ret, gw, uw, dw):
    width, f = inputs.shape[1], gw.shape[1]
    vmem = pl.BlockSpec(memory_space=pltpu.VMEM)
    hbm = pl.BlockSpec(memory_space=pl.ANY)
    dma = pltpu.SemaphoreType.DMA
    n = len(UNITS)
    parts = min(pieces for _, pieces in GROUPS)
    per_group = []
    for slots, pieces in GROUPS:
        r, dc = PEERS * slots, width // pieces
        rows = PLANE * r
        per_group.append([
            ((2, pieces, PLANE, r, dc), BF16),
            ((2, rows, dc), BF16),
            ((rows, 4 * f), F32),
            ((rows, 2 * f), F32),
            ((rows, 2 * f), BF16),
            ((rows, 4 * f), BF16),
            ((2, pieces, PLANE, r, dc), BF16),
            ((2, pieces, 2, 2, r, dc), BF16),
            ((2, pieces, 2, RING, r, dc), BF16),
            ((2, pieces, RING, r, dc), BF16),
            ((2, pieces, 2, r, dc // 2), BF16),
            ((2, pieces, 2, r, dc), BF16),
            ((2 * r, dc), F32),
        ])
    out = jax.ShapeDtypeStruct(inputs.shape, BF16)
    return pl.pallas_call(
        moe_kernel,
        out_shape=(out, out),
        in_specs=[vmem] * 7 + [hbm] * 3,
        out_specs=(vmem, vmem),
        scratch_shapes=[
            pltpu.VMEM((16, width), F32),
            pltpu.VMEM((BLOCK, width), BF16),
            pltpu.VMEM((BLOCK, width), BF16),
            pltpu.VMEM((BLOCK, width), BF16),
            pltpu.VMEM((BLOCK, width), BF16),
            pltpu.VMEM((8, width), BF16),
            pltpu.VMEM((16, PEERS * 8), F32),
            pltpu.VMEM((len(GROUPS), PEERS, BLOCK, width), BF16),
            pltpu.VMEM((len(GROUPS), PEERS, BLOCK, width), BF16),
            pltpu.VMEM((len(GROUPS), PEERS, BLOCK, width), BF16),
            pltpu.VMEM((len(GROUPS), PEERS, BLOCK, width), BF16),
            pltpu.VMEM((4 * f, width), BF16),
            pltpu.VMEM((2 * f, width), BF16),
            *[pltpu.VMEM(*group[i]) for i in range(13) for group in per_group],
            dma((3,)),
            dma((2,)),
            dma((2, parts)),
            dma((n,)),
            dma((n,)),
            dma((n,)),
            dma((n, 2, 2)),
            dma((n,)),
            dma((n, 2, 2)),
            dma((n,)),
            dma((n,)),
        ],
        compiler_params=pltpu.CompilerParams(
            collective_id=0, has_side_effects=True, vmem_limit_bytes=58 << 20
        ),
    )(inputs, conv, ids, gate_values, cot, sel, ret, gw, uw, dw)


def row_maps():
    sel = []
    ret = np.zeros((len(GROUPS), PEERS * 8, 2 * PEERS * GROUPS[0][0]), ml_dtypes.bfloat16)
    for g, (slots, _) in enumerate(GROUPS):
        r = PEERS * slots
        m = np.zeros((2 * r, PEERS * 8), ml_dtypes.bfloat16)
        for a in range(2):
            for s in range(PEERS):
                for i in range(slots):
                    m[a * r + s * slots + i, s * 8 + a * slots + i] = 1
        sel.append(m)
        ret[g, :, : 2 * r] = m.T
    return jnp.asarray(np.concatenate(sel)), jnp.asarray(ret.reshape(-1, ret.shape[-1]))


def per_device(
    inputs, conv_weight, expert_ids, gate_values, cotangent, gate_weight, up_weight, down_weight
):
    sel, ret = row_maps()
    return moe(
        inputs, conv_weight, expert_ids.T, gate_values.T, cotangent, sel, ret,
        jnp.swapaxes(gate_weight, 1, 2), jnp.swapaxes(up_weight, 1, 2), down_weight,
    )


def solution(mesh):
    in_specs = (
        P(("exp", "tp"), None),
        P(),
        P(("exp", "tp"), None),
        P(("exp", "tp"), None),
        P(("exp", "tp"), None),
        P("exp", None, "tp"),
        P("exp", None, "tp"),
        P("exp", "tp", None),
    )
    out_specs = (P(("exp", "tp"), None), P(("exp", "tp"), None))
    return jax.shard_map(
        per_device, mesh=mesh, in_specs=in_specs, out_specs=out_specs, check_vma=False
    )
```

```python
import jax
import jax.numpy as jnp
import ml_dtypes
import numpy as np
from jax import lax
from jax.experimental import pallas as pl
from jax.experimental.pallas import tpu as pltpu
from jax.sharding import PartitionSpec as P

MESH = pl.DeviceIdType.MESH
BF16, F32 = jnp.bfloat16, jnp.float32
RING = 4
PLANE = RING * RING
CORES = 2
SLOTS = 3
PEERS = 8
BLOCK = 4
TAPS = 4
TILE = 1024
GROUPS = ((2, 2), (1, 2))
UNITS = [(g, k) for g, (_, pieces) in enumerate(GROUPS) for k in range(pieces)]
NT = (((1,), (1,)), ((), ()))


def moe_kernel(
    inputs, conv, ids, gate_values, cot, sel, ret, gw, uw, dw, result, grad,
    ext, halo_out, halo_in, back_out, back_in, mixed, gates, pk, xr, pk2, yr, wgu, wd, *rest,
):
    per_group, sems = rest[: 13 * len(GROUPS)], rest[13 * len(GROUPS) :]
    buf, lhs, acc_gu, acc_b, turned, act, res, rel, ful, part, rel2, ful2, fin = (
        per_group[i * len(GROUPS) : (i + 1) * len(GROUPS)] for i in range(13)
    )
    w_sem, h_sem, b_sem, x_send, x_recv, g_send, g_recv, r_send, r_recv, y_send, y_recv = sems
    width = inputs.shape[1]
    f = gw.shape[1]

    x, t = lax.axis_index("exp"), lax.axis_index("tp")
    n_exp, n_tp = PEERS // CORES, PLANE * CORES
    z, y, c = t // (RING * CORES), (t // CORES) % RING, t % CORES
    q = x * CORES + c
    here, devices = x * n_tp + t, n_exp * n_tp

    def rows_of(g):
        return PEERS * GROUPS[g][0]

    def cols_of(u):
        g, k = UNITS[u]
        dc = width // GROUPS[g][1]
        return pl.ds(k * dc, dc)

    def device(x, z, y, c):
        return (x, (z * RING + y) * CORES + c)

    def step_y(by):
        return device(x, z, (y + by) % RING, c)

    def step_z(by):
        return device(x, (z + by) % RING, y, c)

    def line(by):
        v = (here + by) % devices
        return (v // n_tp, v % n_tp)

    axes = ((y, z), (z, y))
    steps = ((step_y, step_z), (step_z, step_y))
    place = [axes[a][1] * RING + axes[a][0] for a in range(2)]

    def remote(src, dst, send_sem, recv_sem, to):
        pltpu.make_async_remote_copy(
            src_ref=src, dst_ref=dst, send_sem=send_sem, recv_sem=recv_sem,
            device_id=to, device_id_type=MESH,
        ).start()

    def wait(sem, like):
        pltpu.make_async_copy(like, like, sem).wait()

    peers = []
    for dx in range(n_exp):
        for dcore in range(CORES):
            if dx or dcore:
                px, pc = (x + dx) % n_exp, (c + dcore) % CORES
                peers.append((px * CORES + pc, device(px, z, y, pc)))
    barrier = pltpu.get_barrier_semaphore()
    partners = [to for _, to in peers] + [s(by) for s in steps[0] for by in (1, -1)]
    partners += [line(1), line(-1)]
    for to in partners:
        pl.semaphore_signal(barrier, inc=1, device_id=to, device_id_type=MESH)

    own = inputs[...].astype(F32)
    ext[8:16, :] = own
    halo_out[...] = own[4:8].astype(BF16)

    r = lax.broadcasted_iota(jnp.int32, (PEERS * 8, 8), 0)
    expert, row = r >> 3, r & 7
    before = lax.broadcasted_iota(jnp.int32, (8, 8), 0) < lax.broadcasted_iota(jnp.int32, (8, 8), 1)
    named = [(expert == ids[k : k + 1, :]).astype(F32) for k in range(2)]
    earlier = jnp.dot(named[0] + named[1], before.astype(F32), preferred_element_type=F32)
    at = [
        jnp.where(row == 4, 2, jnp.where(row < 2, row, -1)),
        jnp.where(row == 5, 2, jnp.where((row == 2) | (row == 3), row - 2, -1)),
    ]
    hit = [(earlier == at[a].astype(F32)).astype(F32) for a in range(2)]
    disp = [((named[0] + named[1]) * hit[a]).astype(BF16) for a in range(2)]
    gate = named[0] * gate_values[0:1, :] + named[1] * gate_values[1:2, :]
    same = lax.broadcasted_iota(jnp.int32, (8, 8), 0) == lax.broadcasted_iota(jnp.int32, (8, 8), 1)
    for a in range(2):
        gates[a * 8 : (a + 1) * 8, :] = lax.dot_general(
            same.astype(F32), gate * hit[a], NT,
            preferred_element_type=F32, precision=lax.Precision.HIGHEST,
        )

    pl.semaphore_wait(barrier, len(partners))
    remote(halo_out, halo_in, h_sem.at[0], h_sem.at[1], line(1))
    wait(h_sem.at[1], halo_in)
    ext[4:8, :] = jnp.where(here == 0, 0.0, halo_in[...].astype(F32))
    total = own
    for j in range(TAPS):
        total = total + conv[j : j + 1, :] * ext[8 - j : 16 - j, :]
    mixed[...] = total.astype(BF16)
    packed = jnp.dot(disp[0], mixed[...], preferred_element_type=F32)
    packed = packed + jnp.dot(disp[1], cot[...], preferred_element_type=F32)
    packed = packed.reshape(PEERS, 8, width)
    pk[0] = packed[:, :BLOCK].astype(BF16)
    pk[1] = packed[:, BLOCK:].astype(BF16)

    for u, (g, _) in enumerate(UNITS):
        cols = cols_of(u)
        for p, to in peers:
            remote(pk.at[g, p, :, cols], xr.at[g, q, :, cols], x_send.at[u], x_recv.at[u], to)
    for g in range(len(GROUPS)):
        xr[g, q] = pk[g, q]

    sibling = device(x, z, y, 1 - c)
    for w, into, first in ((gw, wgu, 0), (uw, wgu, 2 * f), (dw, wd, 0)):
        pltpu.make_async_copy(w.at[c], into.at[pl.ds(first, f)], w_sem.at[0]).start()
        remote(
            w.at[1 - c], into.at[pl.ds(first + f, f)], w_sem.at[1], w_sem.at[2], sibling
        )

    def gather_view(a, u, phase, j, h=None):
        g, k = UNITS[u]
        if phase == 0:
            v = buf[g].at[a, k, axes[a][1] * RING + j]
            half = width // GROUPS[g][1] // 2
            return v if h is None else v.at[:, pl.ds(h * half, half)]
        return buf[g].at[a, k, pl.ds(j * RING, RING) if h is None else pl.ds(j * RING + 2 * h, 2)]

    def blocks(u, n):
        g, k = UNITS[u]
        return buf[g].at[0, k, pl.ds(0, n)]

    def gather_send(u, phase):
        for a in range(2):
            v = gather_view(a, u, phase, axes[a][phase])
            for by in (1, -1):
                remote(v, v, g_send.at[u], g_recv.at[u, phase, 0], steps[a][phase](by))

    def gather_relay(u, phase):
        wait(g_recv.at[u, phase, 0], blocks(u, (4, 16)[phase]))
        for a in range(2):
            for h, by in ((0, 1), (1, -1)):
                v = gather_view(a, u, phase, (axes[a][phase] - by) % RING, h)
                remote(v, v, g_send.at[u], g_recv.at[u, phase, 1], steps[a][phase](by))

    def gather_wait(u, phase):
        wait(g_recv.at[u, phase, 1], blocks(u, (2, 8)[phase]))

    def select(u):
        g, k = UNITS[u]
        cols, n = cols_of(u), rows_of(g)
        wait(x_recv.at[u], xr.at[g, pl.ds(0, PEERS - 1), :, cols])
        got = xr[g, :, :, cols].astype(F32)
        got = jnp.concatenate([got, jnp.zeros_like(got)], 1)
        got = got.reshape(PEERS * 8, got.shape[-1]).astype(BF16)
        first = sum(2 * rows_of(i) for i in range(g))
        mine = jnp.dot(sel[first : first + 2 * n, :], got, preferred_element_type=F32)
        for a in range(2):
            buf[g][a, k, place[a]] = mine[a * n : (a + 1) * n].astype(BF16)

    def products(u):
        g, k = UNITS[u]
        n, cols = rows_of(g), cols_of(u)
        dc, slab = width // GROUPS[g][1], RING * rows_of(g)
        for s in range(RING):
            v = buf[g][0, k, s * RING : (s + 1) * RING].astype(F32)
            lhs[g][0, s * slab : (s + 1) * slab] = v.reshape(slab, dc).astype(BF16)
            v = jnp.stack([buf[g][1, k, j * RING + s] for j in range(RING)], 0).astype(F32)
            lhs[g][1, s * slab : (s + 1) * slab] = v.reshape(slab, dc).astype(BF16)

        def add(acc, a, w, i):
            r = pl.ds(pl.multiple_of(i * 2 * f, 16), 2 * f)
            made = lax.dot_general(w[r, cols], lhs[g][a], NT, preferred_element_type=F32)
            acc[r, :] = made if k == 0 else acc[r, :] + made

        def tile(i, carry):
            add(acc_gu[g], 0, wgu, i)
            return carry

        def tile_b(i, carry):
            add(acc_b[g], 1, wd, i)
            return carry

        lax.fori_loop(0, 2, tile, 0)
        tile_b(0, 0)

    def activate(g):
        m = PLANE * rows_of(g)

        def strip(i, carry):
            at = pl.multiple_of(i * 64, 64)
            r = pl.ds(at, 64)
            gate_pre, up_pre = acc_gu[g][r, :], acc_gu[g][pl.ds(2 * f + at, 64), :]
            back = acc_b[g][r, :]
            s = jax.nn.sigmoid(gate_pre)
            silu = gate_pre * s
            turned[g][r, :] = (silu * up_pre).astype(BF16)
            grad_gate = back * up_pre * s * (1.0 + gate_pre * (1.0 - s))
            turned[g][pl.ds(2 * f + at, 64), :] = grad_gate.astype(BF16)
            turned[g][pl.ds(4 * f + at, 64), :] = (back * silu).astype(BF16)
            return carry

        lax.fori_loop(0, 2 * f // 64, strip, 0)
        one = lax.broadcasted_iota(jnp.int32, (m, m), 0) == lax.broadcasted_iota(jnp.int32, (m, m), 1)
        one = one.astype(F32).astype(BF16)
        for i in range(3):
            r = slice(2 * f * i, 2 * f * (i + 1))
            back = lax.dot_general(one, turned[g][r, :], NT, preferred_element_type=F32)
            act[g][:, r] = back.astype(BF16)

    def outputs(u):
        g, k = UNITS[u]
        n, dc = rows_of(g), width // GROUPS[g][1]

        def tile(i, carry):
            at = pl.multiple_of(i * TILE, TILE)
            cols, to = pl.ds(k * dc + at, TILE), pl.ds(at, TILE)
            forward = jnp.dot(act[g][:, : 2 * f], wd[:, cols], preferred_element_type=F32)
            res[g][0, k, :, :, to] = forward.reshape(PLANE, n, TILE).astype(BF16)
            backward = jnp.dot(act[g][:, 2 * f :], wgu[:, cols], preferred_element_type=F32)
            backward = backward.reshape(RING, RING, n, TILE).astype(BF16)
            for s in range(RING):
                res[g][1, k, s * RING : (s + 1) * RING, :, to] = backward[:, s]
            return carry

        lax.fori_loop(0, dc // TILE, tile, 0)

    def partial(a, u, phase, j, h=None):
        g, k = UNITS[u]
        if phase == 0:
            return res[g].at[
                a, k, pl.ds(j * RING, RING) if h is None else pl.ds(j * RING + 2 * h, 2)
            ]
        v = part[g].at[a, k, j]
        half = width // GROUPS[g][1] // 2
        return v if h is None else v.at[:, pl.ds(h * half, half)]

    def reduce_relay(u, phase):
        g, k = UNITS[u]
        for a in range(2):
            own, to = axes[a][1 - phase], steps[a][1 - phase]
            for h, by in ((0, 1), (1, -1)):
                remote(
                    partial(a, u, phase, (own + 2) % RING, h), (rel, rel2)[phase][g].at[a, k, h],
                    r_send.at[u], r_recv.at[u, phase, 0], to(by),
                )
        if phase == 0:
            for a in range(2):
                own, to = axes[a][1], steps[a][1]
                for h, by in ((0, 1), (1, -1)):
                    remote(
                        partial(a, u, 0, (own + by) % RING, 1 - h),
                        ful[g].at[a, k, h, pl.ds(2 * (1 - h), 2)],
                        r_send.at[u], r_recv.at[u, 0, 1], to(by),
                    )

    def reduce_send(u, phase):
        g, k = UNITS[u]
        wait(r_recv.at[u, phase, 0], blocks(u, (8, 2)[phase]))
        for a in range(2):
            own, to = axes[a][1 - phase], steps[a][1 - phase]
            for h, by in ((0, 1), (1, -1)):
                j = (own + by) % RING
                mine, came = partial(a, u, phase, j, h), (rel, rel2)[phase][g]
                mine[...] = (mine[...].astype(F32) + came[a, k, h].astype(F32)).astype(BF16)
                into = ful[g].at[a, k, h, pl.ds(2 * h, 2)] if phase == 0 else ful2[g].at[a, k, h]
                remote(
                    mine if phase == 0 else partial(a, u, phase, j), into,
                    r_send.at[u], r_recv.at[u, phase, 1], to(by),
                )

    def reduce_sum(u, phase):
        g, k = UNITS[u]
        n = rows_of(g)
        wait(r_recv.at[u, phase, 1], blocks(u, (16, 4)[phase]))
        for a in range(2):
            came = (ful, ful2)[phase][g]
            total = partial(a, u, phase, axes[a][1 - phase])[...].astype(F32)
            total = total + came[a, k, 0].astype(F32) + came[a, k, 1].astype(F32)
            if phase == 0:
                part[g][a, k] = total.astype(BF16)
            else:
                fin[g][a * n : (a + 1) * n, :] = total

    def give_back(u):
        g, _ = UNITS[u]
        cols, n = cols_of(u), 2 * rows_of(g)
        back = ret[g * PEERS * 8 : (g + 1) * PEERS * 8, :n]
        packed = jnp.dot(back, fin[g][...].astype(BF16), preferred_element_type=F32)
        packed = packed.reshape(PEERS, 8, packed.shape[-1])[:, :BLOCK].astype(BF16)
        pk2[g, :, :, cols] = packed
        for p, to in peers:
            remote(pk2.at[g, p, :, cols], yr.at[g, q, :, cols], y_send.at[u], y_recv.at[u], to)
        yr[g, q, :, cols] = pk2[g, q, :, cols]

    parts = min(pieces for _, pieces in GROUPS)
    span = width // parts

    def combine(i):
        cols = pl.ds(i * span, span)
        for u, (g, k) in enumerate(UNITS):
            if k * parts // GROUPS[g][1] == i:
                wait(y_recv.at[u], yr.at[g, pl.ds(0, PEERS - 1), :, cols_of(u)])
        got = [yr[g, :, :, cols].astype(F32) for g in range(len(GROUPS))]
        got = jnp.concatenate(got, 1).reshape(PEERS * 8, span)
        sums = jnp.dot(
            gates[...], got, preferred_element_type=F32, precision=lax.Precision.HIGHEST
        )
        result[:, cols] = (mixed[:, cols].astype(F32) + sums[:8]).astype(BF16)
        grad_mixed = cot[:, cols].astype(F32) + sums[8:]
        ext[0:8, cols] = grad_mixed
        back_out[:, cols] = grad_mixed[:4].astype(BF16)
        remote(
            back_out.at[:, cols], back_in.at[:, cols], b_sem.at[0, i], b_sem.at[1, i], line(-1)
        )

    def finish(i):
        cols = pl.ds(i * span, span)
        wait(b_sem.at[1, i], back_in.at[:, cols])
        ext[8:12, cols] = jnp.where(here == devices - 1, 0.0, back_in[:, cols].astype(F32))
        total = ext[0:8, cols]
        for j in range(TAPS):
            total = total + conv[j : j + 1, cols] * ext[j : j + 8, cols]
        grad[:, cols] = total.astype(BF16)

    n = len(UNITS)
    last = GROUPS[0][1] - 1

    def gather_step(s):
        if s < n:
            select(s)
            gather_send(s, 0)
        if 0 <= s - 1 < n:
            gather_relay(s - 1, 0)
        if 0 <= s - 2 < n:
            gather_wait(s - 2, 0)
            gather_send(s - 2, 1)
        if 0 <= s - 3 < n:
            gather_relay(s - 3, 1)

    def gather_end(u):
        if u == 0:
            wait(w_sem.at[0], wgu.at[pl.ds(0, 3 * f)])
            wait(w_sem.at[2], wgu.at[pl.ds(0, 3 * f)])
        gather_wait(u, 1)
        products(u)
        g, k = UNITS[u]
        if k + 1 == GROUPS[g][1]:
            activate(g)

    def reduce_step(s):
        if s < n:
            outputs(s)
            reduce_relay(s, 0)
        if 0 <= s - 1 < n:
            reduce_send(s - 1, 0)
        if 0 <= s - 2 < n:
            reduce_sum(s - 2, 0)
            reduce_relay(s - 2, 1)
        if 0 <= s - 3 < n:
            reduce_send(s - 3, 1)
        if 0 <= s - 4 < n:
            reduce_sum(s - 4, 1)
            give_back(s - 4)

    for s in range(last + 5):
        gather_step(s)
        if s >= 4:
            gather_end(s - 4)
    for s in range(n + 4):
        reduce_step(s)
        if last + 5 + s < n + 4:
            gather_step(last + 5 + s)
            gather_end(last + 1 + s)
    for i in range(parts):
        combine(i)
    for i in range(parts):
        finish(i)

    wait(h_sem.at[0], halo_out)
    wait(w_sem.at[1], wgu.at[pl.ds(0, 3 * f)])
    for i in range(parts):
        wait(b_sem.at[0, i], back_out.at[:, pl.ds(i * span, span)])
    for u, (g, k) in enumerate(UNITS):
        wait(x_send.at[u], xr.at[g, pl.ds(0, PEERS - 1), :, cols_of(u)])
        wait(y_send.at[u], yr.at[g, pl.ds(0, PEERS - 1), :, cols_of(u)])
        wait(g_send.at[u], buf[g].at[:, k, pl.ds(0, PLANE - 1)])
        wait(r_send.at[u], res[g].at[:, k, pl.ds(0, PLANE - 1)])


def moe(inputs, conv, ids, gate_values, cot, sel, ret, gw, uw, dw):
    width, f = inputs.shape[1], gw.shape[1]
    vmem = pl.BlockSpec(memory_space=pltpu.VMEM)
    hbm = pl.BlockSpec(memory_space=pl.ANY)
    dma = pltpu.SemaphoreType.DMA
    n = len(UNITS)
    parts = min(pieces for _, pieces in GROUPS)
    per_group = []
    for slots, pieces in GROUPS:
        r, dc = PEERS * slots, width // pieces
        rows = PLANE * r
        per_group.append([
            ((2, pieces, PLANE, r, dc), BF16),
            ((2, rows, dc), BF16),
            ((4 * f, rows), F32),
            ((2 * f, rows), F32),
            ((6 * f, rows), BF16),
            ((rows, 6 * f), BF16),
            ((2, pieces, PLANE, r, dc), BF16),
            ((2, pieces, 2, 2, r, dc), BF16),
            ((2, pieces, 2, RING, r, dc), BF16),
            ((2, pieces, RING, r, dc), BF16),
            ((2, pieces, 2, r, dc // 2), BF16),
            ((2, pieces, 2, r, dc), BF16),
            ((2 * r, dc), F32),
        ])
    out = jax.ShapeDtypeStruct(inputs.shape, BF16)
    return pl.pallas_call(
        moe_kernel,
        out_shape=(out, out),
        in_specs=[vmem] * 7 + [hbm] * 3,
        out_specs=(vmem, vmem),
        scratch_shapes=[
            pltpu.VMEM((16, width), F32),
            pltpu.VMEM((BLOCK, width), BF16),
            pltpu.VMEM((BLOCK, width), BF16),
            pltpu.VMEM((BLOCK, width), BF16),
            pltpu.VMEM((BLOCK, width), BF16),
            pltpu.VMEM((8, width), BF16),
            pltpu.VMEM((16, PEERS * 8), F32),
            pltpu.VMEM((len(GROUPS), PEERS, BLOCK, width), BF16),
            pltpu.VMEM((len(GROUPS), PEERS, BLOCK, width), BF16),
            pltpu.VMEM((len(GROUPS), PEERS, BLOCK, width), BF16),
            pltpu.VMEM((len(GROUPS), PEERS, BLOCK, width), BF16),
            pltpu.VMEM((4 * f, width), BF16),
            pltpu.VMEM((2 * f, width), BF16),
            *[pltpu.VMEM(*group[i]) for i in range(13) for group in per_group],
            dma((3,)),
            dma((2,)),
            dma((2, parts)),
            dma((n,)),
            dma((n,)),
            dma((n,)),
            dma((n, 2, 2)),
            dma((n,)),
            dma((n, 2, 2)),
            dma((n,)),
            dma((n,)),
        ],
        compiler_params=pltpu.CompilerParams(
            collective_id=0, has_side_effects=True, vmem_limit_bytes=58 << 20
        ),
    )(inputs, conv, ids, gate_values, cot, sel, ret, gw, uw, dw)


def row_maps():
    sel = []
    ret = np.zeros((len(GROUPS), PEERS * 8, 2 * PEERS * GROUPS[0][0]), ml_dtypes.bfloat16)
    for g, (slots, _) in enumerate(GROUPS):
        r = PEERS * slots
        m = np.zeros((2 * r, PEERS * 8), ml_dtypes.bfloat16)
        for a in range(2):
            for s in range(PEERS):
                for i in range(slots):
                    m[a * r + s * slots + i, s * 8 + a * slots + i] = 1
        sel.append(m)
        ret[g, :, : 2 * r] = m.T
    return jnp.asarray(np.concatenate(sel)), jnp.asarray(ret.reshape(-1, ret.shape[-1]))


def per_device(
    inputs, conv_weight, expert_ids, gate_values, cotangent, gate_weight, up_weight, down_weight
):
    sel, ret = row_maps()
    return moe(
        inputs, conv_weight, expert_ids.T, gate_values.T, cotangent, sel, ret,
        jnp.swapaxes(gate_weight, 1, 2), jnp.swapaxes(up_weight, 1, 2), down_weight,
    )


def solution(mesh):
    in_specs = (
        P(("exp", "tp"), None),
        P(),
        P(("exp", "tp"), None),
        P(("exp", "tp"), None),
        P(("exp", "tp"), None),
        P("exp", None, "tp"),
        P("exp", None, "tp"),
        P("exp", "tp", None),
    )
    out_specs = (P(("exp", "tp"), None), P(("exp", "tp"), None))
    return jax.shard_map(
        per_device, mesh=mesh, in_specs=in_specs, out_specs=out_specs, check_vma=False
    )
```

```python
import jax
import jax.numpy as jnp
import ml_dtypes
import numpy as np
from jax import lax
from jax.experimental import pallas as pl
from jax.experimental.pallas import tpu as pltpu
from jax.sharding import PartitionSpec as P

MESH = pl.DeviceIdType.MESH
BF16, F32 = jnp.bfloat16, jnp.float32
RING = 4
PLANE = RING * RING
CORES = 2
SLOTS = 3
PEERS = 8
BLOCK = 4
TAPS = 4
TILE = 1024
GROUPS = ((1, 2), (2, 2))
UNITS = [(g, k) for g, (_, pieces) in enumerate(GROUPS) for k in range(pieces)]
NT = (((1,), (1,)), ((), ()))


def moe_kernel(
    inputs, conv, ids, gate_values, cot, sel, ret, gw, uw, dw, result, grad,
    ext, halo_out, halo_in, back_out, back_in, mixed, gates, pk, xr, pk2, yr, wgu, wd, *rest,
):
    per_group, sems = rest[: 13 * len(GROUPS)], rest[13 * len(GROUPS) :]
    buf, lhs, acc_gu, acc_b, turned, act, res, rel, ful, part, rel2, ful2, fin = (
        per_group[i * len(GROUPS) : (i + 1) * len(GROUPS)] for i in range(13)
    )
    w_sem, h_sem, b_sem, x_send, x_recv, g_send, g_recv, r_send, r_recv, y_send, y_recv = sems
    width = inputs.shape[1]
    f = gw.shape[1]

    x, t = lax.axis_index("exp"), lax.axis_index("tp")
    n_exp, n_tp = PEERS // CORES, PLANE * CORES
    z, y, c = t // (RING * CORES), (t // CORES) % RING, t % CORES
    q = x * CORES + c
    here, devices = x * n_tp + t, n_exp * n_tp

    def rows_of(g):
        return PEERS * GROUPS[g][0]

    def cols_of(u):
        g, k = UNITS[u]
        dc = width // GROUPS[g][1]
        return pl.ds(k * dc, dc)

    def device(x, z, y, c):
        return (x, (z * RING + y) * CORES + c)

    def step_y(by):
        return device(x, z, (y + by) % RING, c)

    def step_z(by):
        return device(x, (z + by) % RING, y, c)

    def line(by):
        v = (here + by) % devices
        return (v // n_tp, v % n_tp)

    axes = ((y, z), (z, y))
    steps = ((step_y, step_z), (step_z, step_y))
    place = [axes[a][1] * RING + axes[a][0] for a in range(2)]

    def remote(src, dst, send_sem, recv_sem, to):
        pltpu.make_async_remote_copy(
            src_ref=src, dst_ref=dst, send_sem=send_sem, recv_sem=recv_sem,
            device_id=to, device_id_type=MESH,
        ).start()

    def wait(sem, like):
        pltpu.make_async_copy(like, like, sem).wait()

    peers = []
    for dx in range(n_exp):
        for dcore in range(CORES):
            if dx or dcore:
                px, pc = (x + dx) % n_exp, (c + dcore) % CORES
                peers.append((px * CORES + pc, device(px, z, y, pc)))
    barrier = pltpu.get_barrier_semaphore()
    partners = [to for _, to in peers] + [s(by) for s in steps[0] for by in (1, -1)]
    partners += [line(1), line(-1), step_y(2), step_z(2)]
    for to in partners:
        pl.semaphore_signal(barrier, inc=1, device_id=to, device_id_type=MESH)

    own = inputs[...].astype(F32)
    ext[8:16, :] = own
    halo_out[...] = own[4:8].astype(BF16)

    r = lax.broadcasted_iota(jnp.int32, (PEERS * 8, 8), 0)
    expert, row = r >> 3, r & 7
    before = lax.broadcasted_iota(jnp.int32, (8, 8), 0) < lax.broadcasted_iota(jnp.int32, (8, 8), 1)
    named = [(expert == ids[k : k + 1, :]).astype(F32) for k in range(2)]
    earlier = jnp.dot(named[0] + named[1], before.astype(F32), preferred_element_type=F32)
    at = [
        jnp.where(row == 0, 0, jnp.where((row == 4) | (row == 5), row - 3, -1)),
        jnp.where(row == 1, 0, jnp.where(row > 5, row - 5, -1)),
    ]
    hit = [(earlier == at[a].astype(F32)).astype(F32) for a in range(2)]
    disp = [((named[0] + named[1]) * hit[a]).astype(BF16) for a in range(2)]
    gate = named[0] * gate_values[0:1, :] + named[1] * gate_values[1:2, :]
    same = lax.broadcasted_iota(jnp.int32, (8, 8), 0) == lax.broadcasted_iota(jnp.int32, (8, 8), 1)
    for a in range(2):
        gates[a * 8 : (a + 1) * 8, :] = lax.dot_general(
            same.astype(F32), gate * hit[a], NT,
            preferred_element_type=F32, precision=lax.Precision.HIGHEST,
        )

    pl.semaphore_wait(barrier, len(partners))
    remote(halo_out, halo_in, h_sem.at[0], h_sem.at[1], line(1))
    packed = jnp.dot(disp[1], cot[...], preferred_element_type=F32)
    wait(h_sem.at[1], halo_in)
    ext[4:8, :] = jnp.where(here == 0, 0.0, halo_in[...].astype(F32))
    total = own
    for j in range(TAPS):
        total = total + conv[j : j + 1, :] * ext[8 - j : 16 - j, :]
    mixed[...] = total.astype(BF16)
    packed = packed + jnp.dot(disp[0], mixed[...], preferred_element_type=F32)
    packed = packed.reshape(PEERS, 8, width)
    pk[0] = packed[:, :BLOCK].astype(BF16)
    pk[1] = packed[:, BLOCK:].astype(BF16)

    for u, (g, _) in enumerate(UNITS):
        cols = cols_of(u)
        for p, to in peers:
            remote(pk.at[g, p, :, cols], xr.at[g, q, :, cols], x_send.at[u], x_recv.at[u], to)
    for g in range(len(GROUPS)):
        xr[g, q] = pk[g, q]

    sibling = device(x, z, y, 1 - c)
    for w, into, first in ((gw, wgu, 0), (uw, wgu, 2 * f), (dw, wd, 0)):
        pltpu.make_async_copy(w.at[c], into.at[pl.ds(first, f)], w_sem.at[0]).start()
        remote(
            w.at[1 - c], into.at[pl.ds(first + f, f)], w_sem.at[1], w_sem.at[2], sibling
        )

    def gather_view(a, u, phase, j, h=None):
        g, k = UNITS[u]
        if phase == 0:
            v = buf[g].at[a, k, axes[a][1] * RING + j]
            half = width // GROUPS[g][1] // 2
            return v if h is None else v.at[:, pl.ds(h * half, half)]
        return buf[g].at[a, k, pl.ds(j * RING, RING) if h is None else pl.ds(j * RING + 2 * h, 2)]

    def blocks(u, n):
        g, k = UNITS[u]
        return buf[g].at[0, k, pl.ds(0, n)]

    def direct_gather(u, phase):
        return phase == 0 and u < 1

    def direct_reduce(u, phase):
        return phase == 1 and u == len(UNITS) - 1

    def gather_send(u, phase):
        for a in range(2):
            v = gather_view(a, u, phase, axes[a][phase])
            for by in (1, -1):
                remote(v, v, g_send.at[u], g_recv.at[u, phase, 0], steps[a][phase](by))
            if direct_gather(u, phase):
                remote(v, v, g_send.at[u], g_recv.at[u, phase, 1], steps[a][phase](2))

    def gather_relay(u, phase):
        wait(g_recv.at[u, phase, 0], blocks(u, (4, 16)[phase]))
        if direct_gather(u, phase):
            return
        for a in range(2):
            for h, by in ((0, 1), (1, -1)):
                v = gather_view(a, u, phase, (axes[a][phase] - by) % RING, h)
                remote(v, v, g_send.at[u], g_recv.at[u, phase, 1], steps[a][phase](by))

    def gather_wait(u, phase):
        wait(g_recv.at[u, phase, 1], blocks(u, (2, 8)[phase]))

    def select(u):
        g, k = UNITS[u]
        cols, n = cols_of(u), rows_of(g)
        wait(x_recv.at[u], xr.at[g, pl.ds(0, PEERS - 1), :, cols])
        got = xr[g, :, :, cols].astype(F32)
        got = jnp.concatenate([got, jnp.zeros_like(got)], 1)
        got = got.reshape(PEERS * 8, got.shape[-1]).astype(BF16)
        first = sum(2 * rows_of(i) for i in range(g))
        mine = jnp.dot(sel[first : first + 2 * n, :], got, preferred_element_type=F32)
        for a in range(2):
            buf[g][a, k, place[a]] = mine[a * n : (a + 1) * n].astype(BF16)

    def products(u):
        g, k = UNITS[u]
        n, cols = rows_of(g), cols_of(u)
        dc, slab = width // GROUPS[g][1], RING * rows_of(g)
        for s in range(RING):
            v = buf[g][0, k, s * RING : (s + 1) * RING].astype(F32)
            lhs[g][0, s * slab : (s + 1) * slab] = v.reshape(slab, dc).astype(BF16)
            v = jnp.stack([buf[g][1, k, j * RING + s] for j in range(RING)], 0).astype(F32)
            lhs[g][1, s * slab : (s + 1) * slab] = v.reshape(slab, dc).astype(BF16)

        def add(acc, a, w, i):
            r = pl.ds(pl.multiple_of(i * 2 * f, 16), 2 * f)
            made = lax.dot_general(w[r, cols], lhs[g][a], NT, preferred_element_type=F32)
            acc[r, :] = made if k == 0 else acc[r, :] + made

        def tile(i, carry):
            add(acc_gu[g], 0, wgu, i)
            return carry

        def tile_b(i, carry):
            add(acc_b[g], 1, wd, i)
            return carry

        lax.fori_loop(0, 2, tile, 0)
        tile_b(0, 0)

    def activate(g):
        m = PLANE * rows_of(g)

        def strip(i, carry):
            at = pl.multiple_of(i * 64, 64)
            r = pl.ds(at, 64)
            gate_pre, up_pre = acc_gu[g][r, :], acc_gu[g][pl.ds(2 * f + at, 64), :]
            back = acc_b[g][r, :]
            s = jax.nn.sigmoid(gate_pre)
            silu = gate_pre * s
            turned[g][r, :] = (silu * up_pre).astype(BF16)
            grad_gate = back * up_pre * s * (1.0 + gate_pre * (1.0 - s))
            turned[g][pl.ds(2 * f + at, 64), :] = grad_gate.astype(BF16)
            turned[g][pl.ds(4 * f + at, 64), :] = (back * silu).astype(BF16)
            return carry

        lax.fori_loop(0, 2 * f // 64, strip, 0)
        one = lax.broadcasted_iota(jnp.int32, (m, m), 0) == lax.broadcasted_iota(jnp.int32, (m, m), 1)
        one = one.astype(F32).astype(BF16)
        for i in range(3):
            r = slice(2 * f * i, 2 * f * (i + 1))
            back = lax.dot_general(one, turned[g][r, :], NT, preferred_element_type=F32)
            act[g][:, r] = back.astype(BF16)

    def outputs(u):
        g, k = UNITS[u]
        n, dc = rows_of(g), width // GROUPS[g][1]

        def tile(i, carry):
            at = pl.multiple_of(i * TILE, TILE)
            cols, to = pl.ds(k * dc + at, TILE), pl.ds(at, TILE)
            forward = jnp.dot(act[g][:, : 2 * f], wd[:, cols], preferred_element_type=F32)
            res[g][0, k, :, :, to] = forward.reshape(PLANE, n, TILE).astype(BF16)
            backward = jnp.dot(act[g][:, 2 * f :], wgu[:, cols], preferred_element_type=F32)
            backward = backward.reshape(RING, RING, n, TILE).astype(BF16)
            for s in range(RING):
                res[g][1, k, s * RING : (s + 1) * RING, :, to] = backward[:, s]
            return carry

        lax.fori_loop(0, dc // TILE, tile, 0)

    def partial(a, u, phase, j, h=None):
        g, k = UNITS[u]
        if phase == 0:
            return res[g].at[
                a, k, pl.ds(j * RING, RING) if h is None else pl.ds(j * RING + 2 * h, 2)
            ]
        v = part[g].at[a, k, j]
        half = width // GROUPS[g][1] // 2
        return v if h is None else v.at[:, pl.ds(h * half, half)]

    def reduce_relay(u, phase):
        g, k = UNITS[u]
        for a in range(2):
            own, to = axes[a][1 - phase], steps[a][1 - phase]
            far = direct_reduce(u, phase)
            for h, by in ((0, 1), (1, -1)):
                remote(
                    partial(a, u, phase, (own + 2) % RING, h), (rel, rel2)[phase][g].at[a, k, h],
                    r_send.at[u], r_recv.at[u, phase, 0], to(2 if far else by),
                )
                if far:
                    remote(
                        partial(a, u, phase, (own + by) % RING), ful2[g].at[a, k, h],
                        r_send.at[u], r_recv.at[u, phase, 1], to(by),
                    )
        if phase == 0:
            for a in range(2):
                own, to = axes[a][1], steps[a][1]
                for h, by in ((0, 1), (1, -1)):
                    remote(
                        partial(a, u, 0, (own + by) % RING, 1 - h),
                        ful[g].at[a, k, h, pl.ds(2 * (1 - h), 2)],
                        r_send.at[u], r_recv.at[u, 0, 1], to(by),
                    )

    def reduce_send(u, phase):
        g, k = UNITS[u]
        if direct_reduce(u, phase):
            return
        wait(r_recv.at[u, phase, 0], blocks(u, (8, 2)[phase]))
        for a in range(2):
            own, to = axes[a][1 - phase], steps[a][1 - phase]
            for h, by in ((0, 1), (1, -1)):
                j = (own + by) % RING
                mine, came = partial(a, u, phase, j, h), (rel, rel2)[phase][g]
                mine[...] = (mine[...].astype(F32) + came[a, k, h].astype(F32)).astype(BF16)
                into = ful[g].at[a, k, h, pl.ds(2 * h, 2)] if phase == 0 else ful2[g].at[a, k, h]
                remote(
                    mine if phase == 0 else partial(a, u, phase, j), into,
                    r_send.at[u], r_recv.at[u, phase, 1], to(by),
                )

    def reduce_sum(u, phase):
        g, k = UNITS[u]
        n = rows_of(g)
        wait(r_recv.at[u, phase, 1], blocks(u, (16, 4)[phase]))
        if direct_reduce(u, phase):
            wait(r_recv.at[u, phase, 0], blocks(u, 2))
        for a in range(2):
            came = (ful, ful2)[phase][g]
            total = partial(a, u, phase, axes[a][1 - phase])[...].astype(F32)
            total = total + came[a, k, 0].astype(F32) + came[a, k, 1].astype(F32)
            if direct_reduce(u, phase):
                far = [rel2[g][a, k, h].astype(F32) for h in range(2)]
                total = total + jnp.concatenate(far, 1)
            if phase == 0:
                part[g][a, k] = total.astype(BF16)
            else:
                fin[g][a * n : (a + 1) * n, :] = total

    def give_back(u):
        g, _ = UNITS[u]
        cols, n = cols_of(u), 2 * rows_of(g)
        back = ret[g * PEERS * 8 : (g + 1) * PEERS * 8, :n]
        packed = jnp.dot(back, fin[g][...].astype(BF16), preferred_element_type=F32)
        packed = packed.reshape(PEERS, 8, packed.shape[-1])[:, :BLOCK].astype(BF16)
        pk2[g, :, :, cols] = packed
        for p, to in peers:
            remote(pk2.at[g, p, :, cols], yr.at[g, q, :, cols], y_send.at[u], y_recv.at[u], to)
        yr[g, q, :, cols] = pk2[g, q, :, cols]

    parts = min(pieces for _, pieces in GROUPS)
    span = width // parts

    def combine(i):
        cols = pl.ds(i * span, span)
        for u, (g, k) in enumerate(UNITS):
            if k * parts // GROUPS[g][1] == i:
                wait(y_recv.at[u], yr.at[g, pl.ds(0, PEERS - 1), :, cols_of(u)])
        got = [yr[g, :, :, cols].astype(F32) for g in range(len(GROUPS))]
        got = jnp.concatenate(got, 1).reshape(PEERS * 8, span)
        sums = jnp.dot(
            gates[...], got, preferred_element_type=F32, precision=lax.Precision.HIGHEST
        )
        result[:, cols] = (mixed[:, cols].astype(F32) + sums[:8]).astype(BF16)
        grad_mixed = cot[:, cols].astype(F32) + sums[8:]
        ext[0:8, cols] = grad_mixed
        back_out[:, cols] = grad_mixed[:4].astype(BF16)
        remote(
            back_out.at[:, cols], back_in.at[:, cols], b_sem.at[0, i], b_sem.at[1, i], line(-1)
        )

    def finish(i):
        cols = pl.ds(i * span, span)
        wait(b_sem.at[1, i], back_in.at[:, cols])
        ext[8:12, cols] = jnp.where(here == devices - 1, 0.0, back_in[:, cols].astype(F32))
        total = ext[0:8, cols]
        for j in range(TAPS):
            total = total + conv[j : j + 1, cols] * ext[j : j + 8, cols]
        grad[:, cols] = total.astype(BF16)

    n = len(UNITS)
    last = GROUPS[0][1] - 1

    def gather_step(s):
        if s < n:
            select(s)
            gather_send(s, 0)
        if 0 <= s - 1 < n:
            gather_relay(s - 1, 0)
        if 0 <= s - 2 < n:
            gather_wait(s - 2, 0)
            gather_send(s - 2, 1)
        if 0 <= s - 3 < n:
            gather_relay(s - 3, 1)

    def gather_end(u):
        if u == 0:
            wait(w_sem.at[0], wgu.at[pl.ds(0, 3 * f)])
            wait(w_sem.at[2], wgu.at[pl.ds(0, 3 * f)])
        gather_wait(u, 1)
        products(u)
        g, k = UNITS[u]
        if k + 1 == GROUPS[g][1]:
            activate(g)

    def reduce_step(s):
        if s < n:
            outputs(s)
            reduce_relay(s, 0)
        if 0 <= s - 1 < n:
            reduce_send(s - 1, 0)
        if 0 <= s - 2 < n:
            reduce_sum(s - 2, 0)
            reduce_relay(s - 2, 1)
        if 0 <= s - 3 < n:
            reduce_send(s - 3, 1)
        if 0 <= s - 4 < n:
            reduce_sum(s - 4, 1)
            give_back(s - 4)

    for s in range(last + 5):
        gather_step(s)
        if s >= 4:
            gather_end(s - 4)
    for s in range(n + 4):
        reduce_step(s)
        if last + 5 + s < n + 4:
            gather_step(last + 5 + s)
            gather_end(last + 1 + s)
    for i in range(parts):
        combine(i)
    for i in range(parts):
        finish(i)

    wait(h_sem.at[0], halo_out)
    wait(w_sem.at[1], wgu.at[pl.ds(0, 3 * f)])
    for i in range(parts):
        wait(b_sem.at[0, i], back_out.at[:, pl.ds(i * span, span)])
    for u, (g, k) in enumerate(UNITS):
        wait(x_send.at[u], xr.at[g, pl.ds(0, PEERS - 1), :, cols_of(u)])
        wait(y_send.at[u], yr.at[g, pl.ds(0, PEERS - 1), :, cols_of(u)])
        wait(g_send.at[u], buf[g].at[:, k, pl.ds(0, PLANE - 1)])
        wait(r_send.at[u], res[g].at[:, k, pl.ds(0, PLANE - 1)])


def moe(inputs, conv, ids, gate_values, cot, sel, ret, gw, uw, dw):
    width, f = inputs.shape[1], gw.shape[1]
    vmem = pl.BlockSpec(memory_space=pltpu.VMEM)
    hbm = pl.BlockSpec(memory_space=pl.ANY)
    dma = pltpu.SemaphoreType.DMA
    n = len(UNITS)
    parts = min(pieces for _, pieces in GROUPS)
    per_group = []
    for slots, pieces in GROUPS:
        r, dc = PEERS * slots, width // pieces
        rows = PLANE * r
        per_group.append([
            ((2, pieces, PLANE, r, dc), BF16),
            ((2, rows, dc), BF16),
            ((4 * f, rows), F32),
            ((2 * f, rows), F32),
            ((6 * f, rows), BF16),
            ((rows, 6 * f), BF16),
            ((2, pieces, PLANE, r, dc), BF16),
            ((2, pieces, 2, 2, r, dc), BF16),
            ((2, pieces, 2, RING, r, dc), BF16),
            ((2, pieces, RING, r, dc), BF16),
            ((2, pieces, 2, r, dc // 2), BF16),
            ((2, pieces, 2, r, dc), BF16),
            ((2 * r, dc), F32),
        ])
    out = jax.ShapeDtypeStruct(inputs.shape, BF16)
    return pl.pallas_call(
        moe_kernel,
        out_shape=(out, out),
        in_specs=[vmem] * 7 + [hbm] * 3,
        out_specs=(vmem, vmem),
        scratch_shapes=[
            pltpu.VMEM((16, width), F32),
            pltpu.VMEM((BLOCK, width), BF16),
            pltpu.VMEM((BLOCK, width), BF16),
            pltpu.VMEM((BLOCK, width), BF16),
            pltpu.VMEM((BLOCK, width), BF16),
            pltpu.VMEM((8, width), BF16),
            pltpu.VMEM((16, PEERS * 8), F32),
            pltpu.VMEM((len(GROUPS), PEERS, BLOCK, width), BF16),
            pltpu.VMEM((len(GROUPS), PEERS, BLOCK, width), BF16),
            pltpu.VMEM((len(GROUPS), PEERS, BLOCK, width), BF16),
            pltpu.VMEM((len(GROUPS), PEERS, BLOCK, width), BF16),
            pltpu.VMEM((4 * f, width), BF16),
            pltpu.VMEM((2 * f, width), BF16),
            *[pltpu.VMEM(*group[i]) for i in range(13) for group in per_group],
            dma((3,)),
            dma((2,)),
            dma((2, parts)),
            dma((n,)),
            dma((n,)),
            dma((n,)),
            dma((n, 2, 2)),
            dma((n,)),
            dma((n, 2, 2)),
            dma((n,)),
            dma((n,)),
        ],
        compiler_params=pltpu.CompilerParams(
            collective_id=0, has_side_effects=True, vmem_limit_bytes=58 << 20
        ),
    )(inputs, conv, ids, gate_values, cot, sel, ret, gw, uw, dw)


def row_maps():
    sel = []
    most = max(slots for slots, _ in GROUPS)
    ret = np.zeros((len(GROUPS), PEERS * 8, 2 * PEERS * most), ml_dtypes.bfloat16)
    for g, (slots, _) in enumerate(GROUPS):
        r = PEERS * slots
        m = np.zeros((2 * r, PEERS * 8), ml_dtypes.bfloat16)
        for a in range(2):
            for s in range(PEERS):
                for i in range(slots):
                    m[a * r + s * slots + i, s * 8 + a * slots + i] = 1
        sel.append(m)
        ret[g, :, : 2 * r] = m.T
    return jnp.asarray(np.concatenate(sel)), jnp.asarray(ret.reshape(-1, ret.shape[-1]))


def per_device(
    inputs, conv_weight, expert_ids, gate_values, cotangent, gate_weight, up_weight, down_weight
):
    sel, ret = row_maps()
    return moe(
        inputs, conv_weight, expert_ids.T, gate_values.T, cotangent, sel, ret,
        jnp.swapaxes(gate_weight, 1, 2), jnp.swapaxes(up_weight, 1, 2), down_weight,
    )


def solution(mesh):
    in_specs = (
        P(("exp", "tp"), None),
        P(),
        P(("exp", "tp"), None),
        P(("exp", "tp"), None),
        P(("exp", "tp"), None),
        P("exp", None, "tp"),
        P("exp", None, "tp"),
        P("exp", "tp", None),
    )
    out_specs = (P(("exp", "tp"), None), P(("exp", "tp"), None))
    return jax.shard_map(
        per_device, mesh=mesh, in_specs=in_specs, out_specs=out_specs, check_vma=False
    )
```

```python
import jax
import jax.numpy as jnp
import ml_dtypes
import numpy as np
from jax import lax
from jax.experimental import pallas as pl
from jax.experimental.pallas import tpu as pltpu
from jax.sharding import PartitionSpec as P

MESH = pl.DeviceIdType.MESH
BF16, F32 = jnp.bfloat16, jnp.float32
RING = 4
PLANE = RING * RING
CORES = 2
SLOTS = 3
PEERS = 8
BLOCK = 4
TAPS = 4
TILE = 1024
GROUPS = ((1, 2), (2, 2))
UNITS = [(g, k) for g, (_, pieces) in enumerate(GROUPS) for k in range(pieces)]
NT = (((1,), (1,)), ((), ()))


def moe_kernel(
    inputs, conv, ids, gate_values, cot, sel, ret, gw, uw, dw, result, grad,
    ext, halo_out, halo_in, back_out, back_in, mixed, gates, pk, xr, pk2, yr, wgu, wd, *rest,
):
    per_group, sems = rest[: 13 * len(GROUPS)], rest[13 * len(GROUPS) :]
    buf, lhs, acc_gu, acc_b, turned, act, res, rel, ful, part, rel2, ful2, fin = (
        per_group[i * len(GROUPS) : (i + 1) * len(GROUPS)] for i in range(13)
    )
    w_sem, h_sem, b_sem, x_send, x_recv, g_send, g_recv, r_send, r_recv, y_send, y_recv = sems
    width = inputs.shape[1]
    f = gw.shape[1]

    x, t = lax.axis_index("exp"), lax.axis_index("tp")
    n_exp, n_tp = PEERS // CORES, PLANE * CORES
    z, y, c = t // (RING * CORES), (t // CORES) % RING, t % CORES
    q = x * CORES + c
    here, devices = x * n_tp + t, n_exp * n_tp

    def rows_of(g):
        return PEERS * GROUPS[g][0]

    def cols_of(u):
        g, k = UNITS[u]
        dc = width // GROUPS[g][1]
        return pl.ds(k * dc, dc)

    def device(x, z, y, c):
        return (x, (z * RING + y) * CORES + c)

    def step_y(by):
        return device(x, z, (y + by) % RING, c)

    def step_z(by):
        return device(x, (z + by) % RING, y, c)

    def line(by):
        v = (here + by) % devices
        return (v // n_tp, v % n_tp)

    axes = ((y, z), (z, y))
    steps = ((step_y, step_z), (step_z, step_y))
    place = [axes[a][1] * RING + axes[a][0] for a in range(2)]

    def remote(src, dst, send_sem, recv_sem, to):
        pltpu.make_async_remote_copy(
            src_ref=src, dst_ref=dst, send_sem=send_sem, recv_sem=recv_sem,
            device_id=to, device_id_type=MESH,
        ).start()

    def wait(sem, like):
        pltpu.make_async_copy(like, like, sem).wait()

    peers = []
    for dx in range(n_exp):
        for dcore in range(CORES):
            if dx or dcore:
                px, pc = (x + dx) % n_exp, (c + dcore) % CORES
                peers.append((px * CORES + pc, device(px, z, y, pc)))
    barrier = pltpu.get_barrier_semaphore()
    partners = [to for _, to in peers] + [s(by) for s in steps[0] for by in (1, -1)]
    partners += [line(1), line(-1), step_y(2), step_z(2)]
    for to in partners:
        pl.semaphore_signal(barrier, inc=1, device_id=to, device_id_type=MESH)

    weights = ((gw, wgu, 0), (uw, wgu, 2 * f), (dw, wd, 0))
    for w, into, first in weights:
        pltpu.make_async_copy(w.at[c], into.at[pl.ds(first, f)], w_sem.at[0]).start()

    own = inputs[...].astype(F32)
    ext[8:16, :] = own
    halo_out[...] = own[4:8].astype(BF16)

    r = lax.broadcasted_iota(jnp.int32, (PEERS * 8, 8), 0)
    expert, row = r >> 3, r & 7
    before = lax.broadcasted_iota(jnp.int32, (8, 8), 0) < lax.broadcasted_iota(jnp.int32, (8, 8), 1)
    named = [(expert == ids[k : k + 1, :]).astype(F32) for k in range(2)]
    earlier = jnp.dot(named[0] + named[1], before.astype(F32), preferred_element_type=F32)
    at = [
        jnp.where(row == 0, 0, jnp.where((row == 4) | (row == 5), row - 3, -1)),
        jnp.where(row == 1, 0, jnp.where(row > 5, row - 5, -1)),
    ]
    hit = [(earlier == at[a].astype(F32)).astype(F32) for a in range(2)]
    disp = [((named[0] + named[1]) * hit[a]).astype(BF16) for a in range(2)]
    gate = named[0] * gate_values[0:1, :] + named[1] * gate_values[1:2, :]
    pl.semaphore_wait(barrier, len(partners))
    remote(halo_out, halo_in, h_sem.at[0], h_sem.at[1], line(1))
    packed = jnp.dot(disp[1], cot[...], preferred_element_type=F32)
    wait(h_sem.at[1], halo_in)
    ext[4:8, :] = jnp.where(here == 0, 0.0, halo_in[...].astype(F32))
    total = own
    for j in range(TAPS):
        total = total + conv[j : j + 1, :] * ext[8 - j : 16 - j, :]
    mixed[...] = total.astype(BF16)
    packed = packed + jnp.dot(disp[0], mixed[...], preferred_element_type=F32)
    packed = packed.reshape(PEERS, 8, width)
    pk[0] = packed[:, :BLOCK].astype(BF16)
    pk[1] = packed[:, BLOCK:].astype(BF16)

    for u, (g, _) in enumerate(UNITS):
        cols = cols_of(u)
        for p, to in peers:
            remote(pk.at[g, p, :, cols], xr.at[g, q, :, cols], x_send.at[u], x_recv.at[u], to)
    for g in range(len(GROUPS)):
        xr[g, q] = pk[g, q]

    sibling = device(x, z, y, 1 - c)
    for w, into, first in weights:
        remote(
            w.at[1 - c], into.at[pl.ds(first + f, f)], w_sem.at[1], w_sem.at[2], sibling
        )

    same = lax.broadcasted_iota(jnp.int32, (8, 8), 0) == lax.broadcasted_iota(jnp.int32, (8, 8), 1)
    for a in range(2):
        gates[a * 8 : (a + 1) * 8, :] = lax.dot_general(
            same.astype(F32), gate * hit[a], NT,
            preferred_element_type=F32, precision=lax.Precision.HIGHEST,
        )

    def gather_view(a, u, phase, j, h=None):
        g, k = UNITS[u]
        if phase == 0:
            v = buf[g].at[a, k, axes[a][1] * RING + j]
            half = width // GROUPS[g][1] // 2
            return v if h is None else v.at[:, pl.ds(h * half, half)]
        return buf[g].at[a, k, pl.ds(j * RING, RING) if h is None else pl.ds(j * RING + 2 * h, 2)]

    def blocks(u, n):
        g, k = UNITS[u]
        return buf[g].at[0, k, pl.ds(0, n)]

    def direct_gather(u, phase):
        return phase == 0 and u < 1

    def direct_reduce(u, phase):
        return phase == 1 and u == len(UNITS) - 1

    def gather_send(u, phase):
        for a in range(2):
            v = gather_view(a, u, phase, axes[a][phase])
            for by in (1, -1):
                remote(v, v, g_send.at[u], g_recv.at[u, phase, 0], steps[a][phase](by))
            if direct_gather(u, phase):
                remote(v, v, g_send.at[u], g_recv.at[u, phase, 1], steps[a][phase](2))

    def gather_relay(u, phase):
        wait(g_recv.at[u, phase, 0], blocks(u, (4, 16)[phase]))
        if direct_gather(u, phase):
            return
        for a in range(2):
            for h, by in ((0, 1), (1, -1)):
                v = gather_view(a, u, phase, (axes[a][phase] - by) % RING, h)
                remote(v, v, g_send.at[u], g_recv.at[u, phase, 1], steps[a][phase](by))

    def gather_wait(u, phase):
        wait(g_recv.at[u, phase, 1], blocks(u, (2, 8)[phase]))

    def select(u):
        g, k = UNITS[u]
        cols, n = cols_of(u), rows_of(g)
        wait(x_recv.at[u], xr.at[g, pl.ds(0, PEERS - 1), :, cols])
        got = xr[g, :, :, cols].astype(F32)
        got = jnp.concatenate([got, jnp.zeros_like(got)], 1)
        got = got.reshape(PEERS * 8, got.shape[-1]).astype(BF16)
        first = sum(2 * rows_of(i) for i in range(g))
        mine = jnp.dot(sel[first : first + 2 * n, :], got, preferred_element_type=F32)
        for a in range(2):
            buf[g][a, k, place[a]] = mine[a * n : (a + 1) * n].astype(BF16)

    def products(u):
        g, k = UNITS[u]
        n, cols = rows_of(g), cols_of(u)
        dc, slab = width // GROUPS[g][1], RING * rows_of(g)
        for s in range(RING):
            v = buf[g][0, k, s * RING : (s + 1) * RING].astype(F32)
            lhs[g][0, s * slab : (s + 1) * slab] = v.reshape(slab, dc).astype(BF16)
            v = jnp.stack([buf[g][1, k, j * RING + s] for j in range(RING)], 0).astype(F32)
            lhs[g][1, s * slab : (s + 1) * slab] = v.reshape(slab, dc).astype(BF16)

        def add(acc, a, w, i):
            r = pl.ds(pl.multiple_of(i * 2 * f, 16), 2 * f)
            made = lax.dot_general(w[r, cols], lhs[g][a], NT, preferred_element_type=F32)
            acc[r, :] = made if k == 0 else acc[r, :] + made

        def tile(i, carry):
            add(acc_gu[g], 0, wgu, i)
            return carry

        def tile_b(i, carry):
            add(acc_b[g], 1, wd, i)
            return carry

        lax.fori_loop(0, 2, tile, 0)
        tile_b(0, 0)

    def activate(g):
        m = PLANE * rows_of(g)

        def strip(i, carry):
            at = pl.multiple_of(i * 64, 64)
            r = pl.ds(at, 64)
            gate_pre, up_pre = acc_gu[g][r, :], acc_gu[g][pl.ds(2 * f + at, 64), :]
            back = acc_b[g][r, :]
            s = jax.nn.sigmoid(gate_pre)
            silu = gate_pre * s
            turned[g][r, :] = (silu * up_pre).astype(BF16)
            grad_gate = back * up_pre * s * (1.0 + gate_pre * (1.0 - s))
            turned[g][pl.ds(2 * f + at, 64), :] = grad_gate.astype(BF16)
            turned[g][pl.ds(4 * f + at, 64), :] = (back * silu).astype(BF16)
            return carry

        lax.fori_loop(0, 2 * f // 64, strip, 0)
        one = lax.broadcasted_iota(jnp.int32, (m, m), 0) == lax.broadcasted_iota(jnp.int32, (m, m), 1)
        one = one.astype(F32).astype(BF16)
        for i in range(3):
            r = slice(2 * f * i, 2 * f * (i + 1))
            back = lax.dot_general(one, turned[g][r, :], NT, preferred_element_type=F32)
            act[g][:, r] = back.astype(BF16)

    def outputs(u):
        g, k = UNITS[u]
        n, dc = rows_of(g), width // GROUPS[g][1]

        def tile(i, carry):
            at = pl.multiple_of(i * TILE, TILE)
            cols, to = pl.ds(k * dc + at, TILE), pl.ds(at, TILE)
            forward = jnp.dot(act[g][:, : 2 * f], wd[:, cols], preferred_element_type=F32)
            res[g][0, k, :, :, to] = forward.reshape(PLANE, n, TILE).astype(BF16)
            backward = jnp.dot(act[g][:, 2 * f :], wgu[:, cols], preferred_element_type=F32)
            backward = backward.reshape(RING, RING, n, TILE).astype(BF16)
            for s in range(RING):
                res[g][1, k, s * RING : (s + 1) * RING, :, to] = backward[:, s]
            return carry

        lax.fori_loop(0, dc // TILE, tile, 0)

    def partial(a, u, phase, j, h=None):
        g, k = UNITS[u]
        if phase == 0:
            return res[g].at[
                a, k, pl.ds(j * RING, RING) if h is None else pl.ds(j * RING + 2 * h, 2)
            ]
        v = part[g].at[a, k, j]
        half = width // GROUPS[g][1] // 2
        return v if h is None else v.at[:, pl.ds(h * half, half)]

    def reduce_relay(u, phase):
        g, k = UNITS[u]
        for a in range(2):
            own, to = axes[a][1 - phase], steps[a][1 - phase]
            far = direct_reduce(u, phase)
            for h, by in ((0, 1), (1, -1)):
                remote(
                    partial(a, u, phase, (own + 2) % RING, h), (rel, rel2)[phase][g].at[a, k, h],
                    r_send.at[u], r_recv.at[u, phase, 0], to(2 if far else by),
                )
                if far:
                    remote(
                        partial(a, u, phase, (own + by) % RING), ful2[g].at[a, k, h],
                        r_send.at[u], r_recv.at[u, phase, 1], to(by),
                    )
        if phase == 0:
            for a in range(2):
                own, to = axes[a][1], steps[a][1]
                for h, by in ((0, 1), (1, -1)):
                    remote(
                        partial(a, u, 0, (own + by) % RING, 1 - h),
                        ful[g].at[a, k, h, pl.ds(2 * (1 - h), 2)],
                        r_send.at[u], r_recv.at[u, 0, 1], to(by),
                    )

    def reduce_send(u, phase):
        g, k = UNITS[u]
        if direct_reduce(u, phase):
            return
        wait(r_recv.at[u, phase, 0], blocks(u, (8, 2)[phase]))
        for a in range(2):
            own, to = axes[a][1 - phase], steps[a][1 - phase]
            for h, by in ((0, 1), (1, -1)):
                j = (own + by) % RING
                mine, came = partial(a, u, phase, j, h), (rel, rel2)[phase][g]
                mine[...] = (mine[...].astype(F32) + came[a, k, h].astype(F32)).astype(BF16)
                into = ful[g].at[a, k, h, pl.ds(2 * h, 2)] if phase == 0 else ful2[g].at[a, k, h]
                remote(
                    mine if phase == 0 else partial(a, u, phase, j), into,
                    r_send.at[u], r_recv.at[u, phase, 1], to(by),
                )

    def reduce_sum(u, phase):
        g, k = UNITS[u]
        n = rows_of(g)
        wait(r_recv.at[u, phase, 1], blocks(u, (16, 4)[phase]))
        if direct_reduce(u, phase):
            wait(r_recv.at[u, phase, 0], blocks(u, 2))
        for a in range(2):
            came = (ful, ful2)[phase][g]
            total = partial(a, u, phase, axes[a][1 - phase])[...].astype(F32)
            total = total + came[a, k, 0].astype(F32) + came[a, k, 1].astype(F32)
            if direct_reduce(u, phase):
                far = [rel2[g][a, k, h].astype(F32) for h in range(2)]
                total = total + jnp.concatenate(far, 1)
            if phase == 0:
                part[g][a, k] = total.astype(BF16)
            else:
                fin[g][a * n : (a + 1) * n, :] = total

    def give_back(u):
        g, _ = UNITS[u]
        cols, n = cols_of(u), 2 * rows_of(g)
        back = ret[g * PEERS * 8 : (g + 1) * PEERS * 8, :n]
        packed = jnp.dot(back, fin[g][...].astype(BF16), preferred_element_type=F32)
        packed = packed.reshape(PEERS, 8, packed.shape[-1])[:, :BLOCK].astype(BF16)
        pk2[g, :, :, cols] = packed
        for p, to in peers:
            remote(pk2.at[g, p, :, cols], yr.at[g, q, :, cols], y_send.at[u], y_recv.at[u], to)
        yr[g, q, :, cols] = pk2[g, q, :, cols]

    parts = min(pieces for _, pieces in GROUPS)
    span = width // parts

    def combine(i):
        cols = pl.ds(i * span, span)
        for u, (g, k) in enumerate(UNITS):
            if k * parts // GROUPS[g][1] == i:
                wait(y_recv.at[u], yr.at[g, pl.ds(0, PEERS - 1), :, cols_of(u)])
        got = [yr[g, :, :, cols].astype(F32) for g in range(len(GROUPS))]
        got = jnp.concatenate(got, 1).reshape(PEERS * 8, span)
        sums = jnp.dot(
            gates[...], got, preferred_element_type=F32, precision=lax.Precision.HIGHEST
        )
        result[:, cols] = (mixed[:, cols].astype(F32) + sums[:8]).astype(BF16)
        grad_mixed = cot[:, cols].astype(F32) + sums[8:]
        ext[0:8, cols] = grad_mixed
        back_out[:, cols] = grad_mixed[:4].astype(BF16)
        remote(
            back_out.at[:, cols], back_in.at[:, cols], b_sem.at[0, i], b_sem.at[1, i], line(-1)
        )

    def finish(i):
        cols = pl.ds(i * span, span)
        wait(b_sem.at[1, i], back_in.at[:, cols])
        ext[8:12, cols] = jnp.where(here == devices - 1, 0.0, back_in[:, cols].astype(F32))
        total = ext[0:8, cols]
        for j in range(TAPS):
            total = total + conv[j : j + 1, cols] * ext[j : j + 8, cols]
        grad[:, cols] = total.astype(BF16)

    n = len(UNITS)
    last = GROUPS[0][1] - 1

    def gather_step(s):
        if s < n:
            select(s)
            gather_send(s, 0)
        if 0 <= s - 1 < n:
            gather_relay(s - 1, 0)
        if 0 <= s - 2 < n:
            gather_wait(s - 2, 0)
            gather_send(s - 2, 1)
        if 0 <= s - 3 < n:
            gather_relay(s - 3, 1)

    def gather_end(u):
        if u == 0:
            wait(w_sem.at[0], wgu.at[pl.ds(0, 3 * f)])
            wait(w_sem.at[2], wgu.at[pl.ds(0, 3 * f)])
        gather_wait(u, 1)
        products(u)
        g, k = UNITS[u]
        if k + 1 == GROUPS[g][1]:
            activate(g)

    def reduce_step(s):
        if s < n:
            outputs(s)
            reduce_relay(s, 0)
        if 0 <= s - 1 < n:
            reduce_send(s - 1, 0)
        if 0 <= s - 2 < n:
            reduce_sum(s - 2, 0)
            reduce_relay(s - 2, 1)
        if 0 <= s - 3 < n:
            reduce_send(s - 3, 1)
        if 0 <= s - 4 < n:
            reduce_sum(s - 4, 1)
            give_back(s - 4)

    for s in range(last + 5):
        gather_step(s)
        if s >= 4:
            gather_end(s - 4)
    for s in range(n + 4):
        reduce_step(s)
        if last + 5 + s < n + 4:
            gather_step(last + 5 + s)
            gather_end(last + 1 + s)
    for i in range(parts):
        combine(i)
    for i in range(parts):
        finish(i)

    wait(h_sem.at[0], halo_out)
    wait(w_sem.at[1], wgu.at[pl.ds(0, 3 * f)])
    for i in range(parts):
        wait(b_sem.at[0, i], back_out.at[:, pl.ds(i * span, span)])
    for u, (g, k) in enumerate(UNITS):
        wait(x_send.at[u], xr.at[g, pl.ds(0, PEERS - 1), :, cols_of(u)])
        wait(y_send.at[u], yr.at[g, pl.ds(0, PEERS - 1), :, cols_of(u)])
        wait(g_send.at[u], buf[g].at[:, k, pl.ds(0, PLANE - 1)])
        wait(r_send.at[u], res[g].at[:, k, pl.ds(0, PLANE - 1)])


def moe(inputs, conv, ids, gate_values, cot, sel, ret, gw, uw, dw):
    width, f = inputs.shape[1], gw.shape[1]
    vmem = pl.BlockSpec(memory_space=pltpu.VMEM)
    hbm = pl.BlockSpec(memory_space=pl.ANY)
    dma = pltpu.SemaphoreType.DMA
    n = len(UNITS)
    parts = min(pieces for _, pieces in GROUPS)
    per_group = []
    for slots, pieces in GROUPS:
        r, dc = PEERS * slots, width // pieces
        rows = PLANE * r
        per_group.append([
            ((2, pieces, PLANE, r, dc), BF16),
            ((2, rows, dc), BF16),
            ((4 * f, rows), F32),
            ((2 * f, rows), F32),
            ((6 * f, rows), BF16),
            ((rows, 6 * f), BF16),
            ((2, pieces, PLANE, r, dc), BF16),
            ((2, pieces, 2, 2, r, dc), BF16),
            ((2, pieces, 2, RING, r, dc), BF16),
            ((2, pieces, RING, r, dc), BF16),
            ((2, pieces, 2, r, dc // 2), BF16),
            ((2, pieces, 2, r, dc), BF16),
            ((2 * r, dc), F32),
        ])
    out = jax.ShapeDtypeStruct(inputs.shape, BF16)
    return pl.pallas_call(
        moe_kernel,
        out_shape=(out, out),
        in_specs=[vmem] * 7 + [hbm] * 3,
        out_specs=(vmem, vmem),
        scratch_shapes=[
            pltpu.VMEM((16, width), F32),
            pltpu.VMEM((BLOCK, width), BF16),
            pltpu.VMEM((BLOCK, width), BF16),
            pltpu.VMEM((BLOCK, width), BF16),
            pltpu.VMEM((BLOCK, width), BF16),
            pltpu.VMEM((8, width), BF16),
            pltpu.VMEM((16, PEERS * 8), F32),
            pltpu.VMEM((len(GROUPS), PEERS, BLOCK, width), BF16),
            pltpu.VMEM((len(GROUPS), PEERS, BLOCK, width), BF16),
            pltpu.VMEM((len(GROUPS), PEERS, BLOCK, width), BF16),
            pltpu.VMEM((len(GROUPS), PEERS, BLOCK, width), BF16),
            pltpu.VMEM((4 * f, width), BF16),
            pltpu.VMEM((2 * f, width), BF16),
            *[pltpu.VMEM(*group[i]) for i in range(13) for group in per_group],
            dma((3,)),
            dma((2,)),
            dma((2, parts)),
            dma((n,)),
            dma((n,)),
            dma((n,)),
            dma((n, 2, 2)),
            dma((n,)),
            dma((n, 2, 2)),
            dma((n,)),
            dma((n,)),
        ],
        compiler_params=pltpu.CompilerParams(
            collective_id=0, has_side_effects=True, vmem_limit_bytes=58 << 20
        ),
    )(inputs, conv, ids, gate_values, cot, sel, ret, gw, uw, dw)


def row_maps():
    sel = []
    most = max(slots for slots, _ in GROUPS)
    ret = np.zeros((len(GROUPS), PEERS * 8, 2 * PEERS * most), ml_dtypes.bfloat16)
    for g, (slots, _) in enumerate(GROUPS):
        r = PEERS * slots
        m = np.zeros((2 * r, PEERS * 8), ml_dtypes.bfloat16)
        for a in range(2):
            for s in range(PEERS):
                for i in range(slots):
                    m[a * r + s * slots + i, s * 8 + a * slots + i] = 1
        sel.append(m)
        ret[g, :, : 2 * r] = m.T
    return jnp.asarray(np.concatenate(sel)), jnp.asarray(ret.reshape(-1, ret.shape[-1]))


def per_device(
    inputs, conv_weight, expert_ids, gate_values, cotangent, gate_weight, up_weight, down_weight
):
    sel, ret = row_maps()
    return moe(
        inputs, conv_weight, expert_ids.T, gate_values.T, cotangent, sel, ret,
        jnp.swapaxes(gate_weight, 1, 2), jnp.swapaxes(up_weight, 1, 2), down_weight,
    )


def solution(mesh):
    in_specs = (
        P(("exp", "tp"), None),
        P(),
        P(("exp", "tp"), None),
        P(("exp", "tp"), None),
        P(("exp", "tp"), None),
        P("exp", None, "tp"),
        P("exp", None, "tp"),
        P("exp", "tp", None),
    )
    out_specs = (P(("exp", "tp"), None), P(("exp", "tp"), None))
    return jax.shard_map(
        per_device, mesh=mesh, in_specs=in_specs, out_specs=out_specs, check_vma=False
    )
```
